32 devices in a mesh: lvl: 4 (over x, core), gx: 2 (over y), gy: 4 (over z).
Axes of the slice: x: 2, y: 2, z: 4, core: 2. Of those that a mesh axis runs over, the one named last changes fastest.
Arguments:
- initial: float32 [16, 16, 32, 128], P(None, 'gx', 'gy'), may hold values from 0.07 to 1, as said below
- rate_factor: float32 [16, 32, 128], P('gx', 'gy'), may hold values from 0.5 to 2
- diffusivity: float32 [16], replicated, may hold values from 0.3 to 2
- loss_rate: float32 [16], replicated, may hold values from 0.05 to 1.5
- quench: float32 [16, 16], replicated, may hold values from 0 to 0.1
- formation: float32 [16, 16], replicated, may hold values from 0 to 0.1
Outputs:
- final: float32 [4, 16, 16, 32, 128], P('lvl', None, 'gx', 'gy')
The draws below stay inside these ranges and needn't reach their ends.
Inputs may be any that keep to these rules, and one draw needn't show every extreme that they name: `initial`: positive concentrations.
All inputs are finite; a program needn't handle non-finite values.
Results may differ from the reference program's by a relative error of at most 0.0001.
Values sent between devices are 32-bit elements; how exact they have to be, the bound alone decides.
No kernel may reach another device: no remote copies, remote signals or barrier semaphores. Data moves between devices by JAX's collectives and lax.ppermute only.
A program may use at most 64 MiB of HBM per device.

```python
import math
import jax
import jax.numpy as jnp
from jax import lax

C = 16
REACT = 11
NZ = 128
STEPS = 4
SWEEPS = 4
NX = 16
NY = 32
N_LVL = 4


def draw_initial(key, part):
    baseline = jnp.exp(jax.random.uniform(key, (C, NX, NY, NZ), jnp.float32, math.log(0.1), math.log(1.0)))
    return baseline


def steps_of(stream_key, dims, cuts, least, top_value):
    def one(dim, parts):
        heights = jax.random.uniform(jax.random.fold_in(jax.random.fold_in(stream_key, 6), dim), (parts,), jnp.float32, least / len(cuts), top_value / len(cuts))
        return jnp.repeat(jnp.exp(heights), dims[dim] // parts).reshape((-1,) + (1,) * (len(dims) - dim - 1))

    factor_of = one(*cuts[0])
    for cut in cuts[1:]:
        factor_of = factor_of * one(*cut)
    return factor_of


def setup_inputs(seed: int = 0) -> dict:
    key_list = jax.random.split(jax.random.key(seed), 7)
    initial = draw_initial(jax.random.fold_in(key_list[6], 71), 0)
    rate_factor = jnp.clip(jnp.exp(math.log(2.0) - 1.3862944 * jax.random.uniform(key_list[1], (NX, NY, NZ), jnp.float32) ** steps_of(key_list[1], (NX, NY, NZ), ((0, 2), (1, 4)), -0.2, 0.2)), 0.5, 2.0)
    diffusivity = jnp.clip(jnp.exp(jax.random.uniform(key_list[2], (C,), jnp.float32, math.log(0.3), math.log(2.0))), 0.3, 2.0)
    loss_rate = jnp.clip(jnp.exp(jax.random.uniform(key_list[3], (C,), jnp.float32, math.log(0.05), math.log(1.5))), 0.05, 1.5)
    quench = jnp.clip(jax.random.uniform(key_list[4], (C, C), jnp.float32, 0.0, 0.1), 0.0, 0.1)
    formation = jnp.clip(jax.random.uniform(key_list[5], (C, C), jnp.float32, 0.0, 0.1), 0.0, 0.1)
    return {"initial": initial, "rate_factor": rate_factor, "diffusivity": diffusivity, "loss_rate": loss_rate, "quench": quench, "formation": formation}


def pad_rim(values):
    return jnp.pad(values, ((0, 0), (1, 1), (1, 1), (0, 0)))


def conduct(fields, diffusivity):
    return diffusivity[:, None, None, None] * (1.0 + fields * fields)


def face_weights(padded, diffusivity):
    conductance = conduct(padded, diffusivity)
    centre = conductance[:, 1:-1, 1:-1]
    inner_cells = padded[:, 1:-1, 1:-1]
    vertical = conduct(jnp.pad(inner_cells, ((0, 0), (0, 0), (0, 0), (1, 1))), diffusivity)
    west_face = 0.5 * (centre + conductance[:, :-2, 1:-1])
    east_face = 0.5 * (centre + conductance[:, 2:, 1:-1])
    south_face = 0.5 * (centre + conductance[:, 1:-1, :-2])
    north_face = 0.5 * (centre + conductance[:, 1:-1, 2:])
    lower_face = 0.5 * (centre + vertical[..., :-2])
    upper_face = 0.5 * (centre + vertical[..., 2:])
    weight_sum = west_face + east_face + south_face + north_face + lower_face + upper_face
    return (west_face, east_face, south_face, north_face, lower_face, upper_face), weight_sum


def neighbours(padded, coeffs):
    west_face, east_face, south_face, north_face, lower_face, upper_face = coeffs
    inner_cells = padded[:, 1:-1, 1:-1]
    stacked = jnp.pad(inner_cells, ((0, 0), (0, 0), (0, 0), (1, 1)))
    return (west_face * padded[:, :-2, 1:-1] + east_face * padded[:, 2:, 1:-1]
            + south_face * padded[:, 1:-1, :-2] + north_face * padded[:, 1:-1, 2:]
            + lower_face * stacked[..., :-2] + upper_face * stacked[..., 2:])


def chemistry(fields, rate_factor, loss_rate, quench, formation):
    reacting = (jnp.arange(fields.shape[0]) < REACT).astype(jnp.float32)[:, None, None, None]
    squares = jnp.einsum("ij,jxyz->ixyz", quench, fields * fields, precision=lax.Precision.HIGHEST)
    produced = jnp.einsum("ij,jxyz->ixyz", formation, fields, precision=lax.Precision.HIGHEST)
    loss_term = reacting * loss_rate[:, None, None, None] * rate_factor[None] * (1.0 + squares)
    production = reacting * rate_factor[None] * produced
    return loss_term, production


def reference(initial, rate_factor, diffusivity, loss_rate, quench, formation):
    inflows = [jnp.zeros_like(initial) for step_index in range(STEPS)]
    finals = []
    for level_index in range(N_LVL):
        current_state = initial
        outgoing = []
        previous_tendency = jnp.zeros_like(initial)
        carried = jnp.zeros_like(initial)
        for node_index in range(STEPS + 1):
            padded = pad_rim(current_state)
            coeffs, weight_sum = face_weights(padded, diffusivity)
            loss_term, production = chemistry(current_state, rate_factor, loss_rate, quench, formation)
            diffused = neighbours(padded, coeffs) - weight_sum * current_state
            tendency = diffused + production - loss_term * current_state
            if node_index > 0:
                outgoing.append(0.5 * (previous_tendency + tendency) - carried)
            if node_index < STEPS:
                right_side = current_state + production + inflows[node_index]
                denominator = 1.0 + loss_term + weight_sum
                iterate = current_state
                padded_now = padded
                for sweep_index in range(SWEEPS):
                    if sweep_index > 0:
                        padded_now = pad_rim(iterate)
                    iterate = (right_side + neighbours(padded_now, coeffs)) / denominator
                carried = production + (iterate - right_side)
                previous_tendency = tendency
                current_state = iterate
        finals.append(current_state)
        inflows = outgoing
    return jnp.stack(finals)
```

```python
import functools

import jax
import jax.numpy as jnp
from jax import lax
from jax.experimental import pallas as pl
from jax.experimental.pallas import tpu as pltpu
from jax.sharding import PartitionSpec as P

REACT = 11
STEPS = 4
SWEEPS = 4
RIM = SWEEPS - 1
AXES = ("lvl", "gx", "gy")


def split_of(count, rows, cols):
    parts_x = 1
    while parts_x * parts_x < count:
        parts_x *= 2
    parts_y = count // parts_x
    assert parts_x * parts_y == count and rows % parts_x == 0 and cols % parts_y == 0
    assert rows // parts_x >= SWEEPS and cols // parts_y >= SWEEPS
    return parts_x, parts_y


class Layout:
    def __init__(self, rows, cols):
        self.levels, self.gx, self.gy = (lax.axis_size(a) for a in AXES)
        self.parts_x, self.parts_y = split_of(self.levels, rows, cols)
        self.sub_x, self.sub_y = rows // self.parts_x, cols // self.parts_y

    def spot(self, part, gx, gy):
        half = part // self.parts_y
        half = half if gx % 2 == 0 else self.parts_x - 1 - half
        return gx * self.parts_x + half, gy * self.parts_y + part % self.parts_y

    def shifts(self, dx, dy):
        device = {}
        for part in range(self.levels):
            for gx in range(self.gx):
                for gy in range(self.gy):
                    device[self.spot(part, gx, gy)] = (part * self.gx + gx) * self.gy + gy
        return [(d, device[x + dx, y + dy]) for (x, y), d in sorted(device.items()) if (x + dx, y + dy) in device]

    def traced_spot(self):
        part, gx, gy = (lax.axis_index(a) for a in AXES)
        half = part // self.parts_y
        half = jnp.where(gx % 2 == 0, half, self.parts_x - 1 - half)
        return half, part % self.parts_y, gx, gy


def send(value, layout, dx, dy):
    return lax.ppermute(value, AXES, layout.shifts(dx, dy))


def exchange(state, layout, dim, width):
    rows, cols = state.shape[dim], state.shape[dim + 1]
    before = send(lax.slice_in_dim(state, rows - width, rows, axis=dim), layout, 1, 0)
    after = send(lax.slice_in_dim(state, 0, width, axis=dim), layout, -1, 0)
    middle = jnp.concatenate([before, state, after], axis=dim)
    left = send(lax.slice_in_dim(middle, cols - width, cols, axis=dim + 1), layout, 0, 1)
    right = send(lax.slice_in_dim(middle, 0, width, axis=dim + 1), layout, 0, -1)
    return left, middle, right


def halves(x):
    high = x.astype(jnp.bfloat16)
    return high, (x - high.astype(jnp.float32)).astype(jnp.bfloat16)


def matrix_halves(x):
    high = lax.reduce_precision(x, 8, 7)
    return high.astype(jnp.bfloat16), (x - high).astype(jnp.bfloat16)


def product(high, low, x):
    x_high, x_low = halves(x)
    dot = functools.partial(jnp.dot, preferred_element_type=jnp.float32)
    return dot(high, x_high) + (dot(high, x_low) + dot(low, x_high))


def level_pass(u_src, env, node, first, inflow_in, inflow_out, kept_old, kept_new, out):
    u, c, sq, pr, va, vb, wx, wy, wu, wl, rhs, rden, infl = env["scratch"]
    rate, mask, half_d, loss, mats = env["rate"], env["mask"], env["half_d"], env["loss"], env["mats"]
    wide_x, wide_y, fields, nz = u.shape
    rx, ry = wide_x - 2, wide_y - 2
    widths = [s.shape[1] for s in u_src]

    hd = half_d[...]

    def widen(x, carry):
        at = 0
        for strip, width in zip(u_src, widths):
            for y in range(width):
                value = strip[x, y]
                u[x, at + y] = value
                c[x, at + y] = hd + hd * (value * value)
            at += width
        return carry

    lax.fori_loop(0, wide_x, widen, 0)

    def chemistry(i, carry):
        rows = [u[2 * i + 1 + k, 1 : 1 + ry].reshape(ry * fields, nz) for k in range(2)]
        value = jnp.concatenate(rows, axis=1)
        squares = product(mats[0], mats[1], value * value)
        made = product(mats[2], mats[3], value)
        for k in range(2):
            sq[2 * i + k] = squares[:, k * nz : (k + 1) * nz].reshape(ry, fields, nz)
            pr[2 * i + k] = made[:, k * nz : (k + 1) * nz].reshape(ry, fields, nz)
        return carry

    lax.fori_loop(0, rx // 2, chemistry, 0)

    lane = lax.broadcasted_iota(jnp.int32, (fields, nz), 1)
    bottom, top = lane == 0, lane == nz - 1
    lr = loss[...]
    advance = node < STEPS

    def setup(x, carry):
        X = x + 1
        u_here, u_next = u[X, 0], u[X, 1]
        c_here, c_next = c[X, 0], c[X, 1]
        wy_next = c_here + c_next
        for y in range(ry):
            Y = y + 1
            u_prev, u_here, u_next = u_here, u_next, u[X, Y + 1]
            c_here, c_next = c_next, c[X, Y + 1]
            wy_prev, wy_next = wy_next, c_here + c_next
            wx_prev = c_here + c[X - 1, Y]
            wx_next = c_here + c[X + 1, Y]
            w_up = c_here + jnp.where(top, hd, pltpu.roll(c_here, nz - 1, 1))
            w_low = c_here + jnp.where(bottom, hd, pltpu.roll(c_here, 1, 1))
            weights = ((wx_prev + wx_next) + (wy_prev + wy_next)) + (w_up + w_low)
            w_up = jnp.where(top, 0.0, w_up)
            w_low = jnp.where(bottom, 0.0, w_low)
            near = (
                (wx_prev * u[X - 1, Y] + wx_next * u[X + 1, Y])
                + (wy_prev * u_prev + wy_next * u_next)
                + (w_low * pltpu.roll(u_here, 1, 1) + w_up * pltpu.roll(u_here, nz - 1, 1))
            )
            factor = jnp.broadcast_to(rate[x, pl.ds(y, 1), :], (fields, nz))
            made = factor * pr[x, y]
            drop = factor * (lr + sq[x, y]) + weights
            if inflow_out:
                half_t = 0.5 * (near + made - drop * u_here)
            if advance:
                source = u_here + infl[x, y] if inflow_in else u_here
            if inflow_out:
                if not first:
                    infl[x, y] = kept_old[x, y] + (half_t - u_here)
                if advance:
                    kept_new[x, y] = half_t + source
            if advance:
                right = source + made
                inverse = (mask[0, x] * mask[1, y]) / (1.0 + drop)
                rhs[x, y] = right
                rden[x, y] = inverse
                wx[x, y] = wx_next
                wy[x, y] = wy_next
                wu[x, y] = w_up
                wl[x, y] = w_low
                va[x, y] = (right + near) * inverse
        return carry

    lax.fori_loop(0, rx, setup, 0)
    if not advance:
        return

    old, new = va, vb
    for k in range(1, SWEEPS):
        last = k == SWEEPS - 1

        def sweep(x, carry, k=k, old=old, new=new, last=last):
            v_here, v_next = old[x, k - 1], old[x, k]
            w_next = wy[x, k - 1]
            for y in range(k, ry - k):
                v_prev, v_here, v_next = v_here, v_next, old[x, y + 1]
                w_prev, w_next = w_next, wy[x, y]
                near = (
                    (wx[x - 1, y] * old[x - 1, y] + wx[x, y] * old[x + 1, y])
                    + (w_prev * v_prev + w_next * v_next)
                    + (wl[x, y] * pltpu.roll(v_here, 1, 1) + wu[x, y] * pltpu.roll(v_here, nz - 1, 1))
                )
                value = (rhs[x, y] + near) * rden[x, y]
                if last:
                    out[x - k, y - k] = value
                else:
                    new[x, y] = value
            return carry

        lax.fori_loop(k, rx - k, sweep, 0)
        old, new = new, old


def wave(diagonal, levels, shapes, started, moved, rate, mask, half_d, loss, mats, kept):
    active = [p for p in range(levels) if 0 <= diagonal - p <= STEPS and not (p == levels - 1 and diagonal - p == STEPS)]
    going = [p for p in active if diagonal - p < STEPS]
    keepers = [p for p in going if p < levels - 1]
    old = [p for p in active if 0 < diagonal - p and p < levels - 1]
    sub_x, sub_y, fields, nz = shapes
    wide = (sub_x + 2 * SWEEPS, sub_y + 2 * SWEEPS, fields, nz)
    core = (sub_x + 2 * RIM, sub_y + 2 * RIM, fields, nz)
    sources = (list(started) if any(p == diagonal for p in active) else []) + (list(moved) if moved is not None else [])
    n_src = len(sources)

    def kernel(*refs):
        refs = list(refs)
        take = lambda n: [refs.pop(0) for _ in range(n)]
        src = take(n_src)
        rate_ref, mask_ref, half_ref, loss_ref, mats_ref = take(5)
        old_refs = dict(zip(old, take(len(old))))
        (state_ref,) = take(1)
        new_refs = dict(zip(keepers, take(len(keepers))))
        scratch = refs
        env = {"scratch": scratch, "rate": rate_ref, "mask": mask_ref, "half_d": half_ref, "loss": loss_ref, "mats": mats_ref}
        slot = 0
        for p in active:
            node = diagonal - p
            if node == 0:
                strips = src[:3]
            else:
                strips = [r.at[slot] for r in src[n_src - 3 :]]
                slot += 1
            level_pass(
                strips, env, node, node == 0, p > 0, p < levels - 1,
                old_refs.get(p), new_refs.get(p),
                state_ref.at[going.index(p)] if p in going else None,
            )

    vmem = pl.BlockSpec(memory_space=pltpu.VMEM)
    smem = pl.BlockSpec(memory_space=pltpu.SMEM)
    f32 = jnp.float32
    operands = sources + [rate, mask, half_d, loss, mats] + [kept[p] for p in old]
    in_specs = [vmem] * n_src + [vmem, smem, vmem, vmem, vmem] + [vmem] * len(old)
    out_shape = [jax.ShapeDtypeStruct((len(going), sub_x, sub_y, fields, nz), f32)]
    out_shape += [jax.ShapeDtypeStruct(core, f32) for _ in keepers]
    cells = core[0] * core[1] * fields * nz
    results = pl.pallas_call(
        kernel,
        out_shape=out_shape,
        in_specs=in_specs,
        out_specs=[vmem] * len(out_shape),
        scratch_shapes=[pltpu.VMEM(wide, f32)] * 2 + [pltpu.VMEM(core, f32)] * 11,
        compiler_params=pltpu.CompilerParams(vmem_limit_bytes=50 * 2**20),
        cost_estimate=pl.CostEstimate(flops=150 * cells * len(active), bytes_accessed=8 * cells, transcendentals=0),
        name="wave%d" % diagonal,
    )(*operands)
    return going, results[0], dict(zip(keepers, results[1:]))


def inside_mask(layout, half_x, half_y, gx, gy):
    length = max(layout.sub_x, layout.sub_y) + 2 * RIM
    offsets = jnp.arange(length) - RIM
    rows = (gx * layout.parts_x + half_x) * layout.sub_x + offsets
    cols = (gy * layout.parts_y + half_y) * layout.sub_y + offsets
    row_ok = (rows >= 0) & (rows < layout.sub_x * layout.parts_x * layout.gx)
    col_ok = (cols >= 0) & (cols < layout.sub_y * layout.parts_y * layout.gy)
    return jnp.stack([row_ok, col_ok]).astype(jnp.float32)


def on_device(initial, rate_factor, diffusivity, loss_rate, quench, formation):
    fields, rows, cols, nz = initial.shape
    layout = Layout(rows, cols)
    levels = layout.levels
    half_x, half_y, gx, gy = layout.traced_spot()
    sub_x, sub_y = layout.sub_x, layout.sub_y
    row_at, col_at = half_x * sub_x, half_y * sub_y

    own = lax.dynamic_slice(initial, (0, row_at, col_at, 0), (fields, sub_x, sub_y, nz))
    own = jnp.transpose(own, (1, 2, 0, 3))
    started = exchange(own, layout, 0, SWEEPS)
    own_rate = lax.dynamic_slice(rate_factor, (row_at, col_at, 0), (sub_x, sub_y, nz))
    rate = jnp.concatenate(exchange(own_rate, layout, 0, RIM), axis=1)
    mask = inside_mask(layout, half_x, half_y, gx, gy)

    reacting = (jnp.arange(fields) < REACT).astype(jnp.float32)
    half_d = jnp.broadcast_to(0.5 * diffusivity[:, None], (fields, nz))
    loss = jnp.broadcast_to((reacting * loss_rate)[:, None], (fields, nz))
    eye = jnp.eye(sub_y + 2 * RIM, dtype=jnp.float32)
    mats = []
    for matrix in ((reacting * loss_rate)[:, None] * quench, reacting[:, None] * formation):
        mats += matrix_halves(jnp.kron(eye, matrix))
    mats = jnp.stack(mats)

    kept, moved, finals = {}, None, {}
    for diagonal in range(levels + STEPS - 1):
        going, states, kept = wave(
            diagonal, levels, (sub_x, sub_y, fields, nz), started, moved, rate, mask, half_d, loss, mats, kept
        )
        needed = []
        for i, p in enumerate(going):
            done = diagonal - p + 1 == STEPS
            if done:
                finals[p] = states[i]
            if not (done and p == levels - 1):
                needed.append(i)
        if needed:
            moved = exchange(states[needed[0] : needed[-1] + 1], layout, 1, SWEEPS)

    parts = lax.all_to_all(jnp.stack([finals[p] for p in range(levels)]), "lvl", 0, 0, tiled=True)
    parts = parts.reshape(layout.parts_x, layout.parts_y, sub_x, sub_y, fields, nz)
    parts = jnp.where(gx % 2 == 0, parts, parts[::-1])
    return jnp.transpose(parts, (4, 0, 2, 1, 3, 5)).reshape(1, fields, rows, cols, nz)


def solution(mesh):
    in_specs = (P(None, "gx", "gy", None), P("gx", "gy", None), P(), P(), P(), P())
    out_specs = P("lvl", None, "gx", "gy", None)
    return jax.shard_map(
        on_device, mesh=mesh, in_specs=in_specs, out_specs=out_specs, check_vma=False
    )
```

```python
import functools

import jax
import jax.numpy as jnp
from jax import lax
from jax.experimental import pallas as pl
from jax.experimental.pallas import tpu as pltpu
from jax.sharding import PartitionSpec as P

REACT = 11
STEPS = 4
SWEEPS = 4
RIM = SWEEPS - 1
GROUP = 4
AXES = ("lvl", "gx", "gy")


class Plan:
    def __init__(self, rows, cols):
        self.levels, self.gx, self.gy = (lax.axis_size(a) for a in AXES)
        self.rows, self.cols = rows, cols
        self.closed = self.gx <= 2
        parts = self.levels
        if self.closed:
            self.parts_x, self.parts_y = 1, 1
            while parts % (2 * self.parts_y) == 0 and cols // (2 * self.parts_y) >= SWEEPS:
                self.parts_y *= 2
            self.sub_x, self.wide_x = rows * self.gx, rows * self.gx + 2
        else:
            self.parts_x = 1
            while self.parts_x * self.parts_x < parts:
                self.parts_x *= 2
            self.parts_y = parts // self.parts_x
            assert self.parts_x * self.parts_y == parts and rows % self.parts_x == 0
            self.sub_x, self.wide_x = rows // self.parts_x, rows // self.parts_x + 2 * SWEEPS
        assert cols % self.parts_y == 0
        self.sub_y = cols // self.parts_y
        assert min(self.sub_x, self.sub_y) >= SWEEPS
        self.wide_y = self.sub_y + 2 * SWEEPS
        self.core_x, self.core_y = self.wide_x - 2, self.wide_y - 2

    def spot(self, part, gx, gy):
        at_y = gy * self.parts_y + part % self.parts_y
        if self.closed:
            return gx, part // self.parts_y, at_y
        half = part // self.parts_y
        half = half if gx % 2 == 0 else self.parts_x - 1 - half
        return gx * self.parts_x + half, 0, at_y

    def devices(self):
        found = {}
        for part in range(self.levels):
            for gx in range(self.gx):
                for gy in range(self.gy):
                    found[self.spot(part, gx, gy)] = (part * self.gx + gx) * self.gy + gy
        return found

    def column(self, device):
        return device // (self.gx * self.gy) % self.parts_y

    def shifts(self, dx, dy):
        found = self.devices()
        there = lambda s: (s[0] + dx, s[1], s[2] + dy)
        return [(d, found[there(s)]) for s, d in sorted(found.items()) if there(s) in found]


def columns(own, rate, plan):
    half = lax.axis_index("lvl") % plan.parts_y
    gx = lax.axis_index("gx")
    sub, nz = plan.sub_y, own.shape[-1]
    both = jnp.concatenate([own, rate[:, :, None, :]], axis=2) if not plan.closed else None
    if plan.closed:
        cells, planes = own.shape[0] * own.shape[1], own.shape[2]

        def pack(x, r):
            return jnp.concatenate([x.reshape(-1, nz), r.reshape(-1, nz)], axis=0)

        def unpack(packed, x, r):
            return packed[: x.size // nz].reshape(x.shape), packed[x.size // nz :].reshape(r.shape)

        if plan.gx == 2:
            theirs = unpack(lax.ppermute(pack(own, rate), "gx", [(0, 1), (1, 0)]), own, rate)
            own, rate = (
                jnp.where(gx == 0, jnp.concatenate([a, b], axis=0), jnp.concatenate([b, a], axis=0))
                for a, b in zip((own, rate), theirs)
            )
        if plan.parts_y == 2:
            pairs = sorted(
                [(a, b) for a, b in plan.shifts(0, 1) if plan.column(a) == 1]
                + [(a, b) for a, b in plan.shifts(0, -1) if plan.column(a) == 0]
            )
            outer = [jnp.where(half == 1, x[:, -SWEEPS:], x[:, :SWEEPS]) for x in (own, rate)]
            come = unpack(lax.ppermute(pack(*outer), AXES, pairs), *outer)
            wide = []
            for x, o in zip((own, rate), come):
                x_before = jnp.where(half == 0, o, x[:, sub - SWEEPS : sub])
                x_after = jnp.where(half == 0, x[:, sub : sub + SWEEPS], o)
                wide.append((x_before, jnp.where(half == 0, x[:, :sub], x[:, sub:]), x_after))
            return wide
        both = jnp.concatenate([own, rate[:, :, None, :]], axis=2)
    else:
        at = lax.axis_index("lvl") // plan.parts_y
        at = jnp.where(gx % 2 == 0, at, plan.parts_x - 1 - at) * plan.sub_x
        both = lax.dynamic_slice_in_dim(both, at, plan.sub_x, axis=0)
    both = lax.dynamic_slice_in_dim(both, half * sub, sub, axis=1)
    strips = exchange(both[None], plan)
    return [[x[0, :, :, :-1] for x in strips], [x[0, :, :, -1] for x in strips]]


def exchange(states, plan):
    if not plan.closed:
        before = lax.ppermute(states[:, -SWEEPS:], AXES, plan.shifts(1, 0))
        after = lax.ppermute(states[:, :SWEEPS], AXES, plan.shifts(-1, 0))
        states = jnp.concatenate([before, states, after], axis=1)
    before = lax.ppermute(states[:, :, -SWEEPS:], AXES, plan.shifts(0, 1))
    after = lax.ppermute(states[:, :, :SWEEPS], AXES, plan.shifts(0, -1))
    return before, states, after


def halves(x):
    high = x.astype(jnp.bfloat16)
    return high, (x - high.astype(jnp.float32)).astype(jnp.bfloat16)


def product(matrix, x):
    dot = functools.partial(jnp.dot, preferred_element_type=jnp.float32)
    n = matrix.shape[0] // 2
    high, low = halves(x)
    first = dot(matrix, high)
    return first[:n] + (first[n:] + dot(matrix[:n], low))


def level_pass(strips, env, plan, node, inflow_in, inflow_out, kept_old, kept_new, out):
    u, c, chem, va, vb, wx, wy, wu, rhs, rden = env["scratch"]
    rate, mask, half_d, loss, mats = env["rate"], env["mask"], env["half_d"], env["loss"], env["mats"]
    fields, nz = u.shape[2:]
    rx, ry = plan.core_x, plan.core_y
    hd = half_d[...]
    base = 1 if plan.closed else 0
    shrink = 0 if plan.closed else 1

    def conduct(value):
        return hd + hd * (value * value)

    def widen(x, carry):
        at = 0
        for strip in strips:
            for y in range(strip.shape[1]):
                value = strip[x, y]
                u[x + base, at + y] = value
                c[x + base, at + y] = conduct(value)
            at += strip.shape[1]
        return carry

    lax.fori_loop(0, strips[0].shape[0], widen, 0)

    lane = lax.broadcasted_iota(jnp.int32, (fields, nz), 1)
    bottom, top = lane == 0, lane == nz - 1
    lr = loss[...]
    advance = node < STEPS

    def setup(x, k):
        X = x + 1
        u_here, u_next = u[X, 0], u[X, 1]
        c_here, c_next = c[X, 0], c[X, 1]
        wy_next = c_here + c_next
        for y in range(ry):
            Y = y + 1
            u_prev, u_here, u_next = u_here, u_next, u[X, Y + 1]
            c_here, c_next = c_next, c[X, Y + 1]
            wy_prev, wy_next = wy_next, c_here + c_next
            wx_prev = c_here + c[X - 1, Y]
            wx_next = c_here + c[X + 1, Y]
            below = jnp.where(bottom, 0.0, pltpu.roll(u_here, 1, 1))
            above = jnp.where(top, 0.0, pltpu.roll(u_here, nz - 1, 1))
            w_low = c_here + conduct(below)
            w_up = c_here + conduct(above)
            weights = ((wx_prev + wx_next) + (wy_prev + wy_next)) + (w_low + w_up)
            near = (
                (wx_prev * u[X - 1, Y] + wx_next * u[X + 1, Y])
                + (wy_prev * u_prev + wy_next * u_next)
                + (w_low * below + w_up * above)
            )
            factor = jnp.broadcast_to(rate[x, pl.ds(y, 1), :], (fields, nz))
            made = factor * chem[1, k, y]
            drop = factor * (lr + chem[0, k, y]) + weights
            if advance:
                source = u_here + inflow_in[x, y] if inflow_in is not None else u_here
            if inflow_out is not None or kept_new is not None:
                half_t = 0.5 * (near + made - drop * u_here)
            if inflow_out is not None:
                inflow_out[x, y] = kept_old[x, y] + (half_t - u_here)
            if kept_new is not None:
                kept_new[x, y] = half_t + source
            if advance:
                right = source + made
                inverse = (mask[0, x] * mask[1, y]) / (1.0 + drop)
                rhs[x, y] = right
                rden[x, y] = inverse
                wx[X, y] = wx_next
                wy[x, y] = wy_next
                wu[x, y] = jnp.where(top, 0.0, w_up)
                va[X, y] = (right + near) * inverse

    def rows_two(i, carry):
        value = jnp.concatenate([u[2 * i + 1 + k, 1 : 1 + ry].reshape(ry * fields, nz) for k in range(2)], axis=1)
        for j, result in enumerate((product(mats[0], value * value), product(mats[1], value))):
            for k in range(2):
                chem[j, k] = result[:, k * nz : (k + 1) * nz].reshape(ry, fields, nz)
        for k in range(2):
            setup(2 * i + k, k)
        return carry

    lax.fori_loop(0, rx // 2, rows_two, 0)
    if not advance:
        return
    if plan.closed:
        for y in range(ry):
            wx[0, y] = c[0, y + 1] + c[1, y + 1]

    old, new = va, vb
    for k in range(1, SWEEPS):
        lead = k * shrink
        count = rx - 2 * lead
        n = 4 if count % 4 == 0 else 2

        def sweep(i, carry, k=k, old=old, new=new, lead=lead, n=n):
            x = lead + n * i
            X = x + 1
            v_here = [old[X + j, k - 1] for j in range(n)]
            v_next = [old[X + j, k] for j in range(n)]
            w_next = [wy[x + j, k - 1] for j in range(n)]
            for y in range(k, ry - k):
                v_prev, v_here, v_next = v_here, v_next, [old[X + j, y + 1] for j in range(n)]
                w_prev, w_next = w_next, [wy[x + j, y] for j in range(n)]
                rows = [old[X - 1, y]] + v_here + [old[X + n, y]]
                faces = [wx[X - 1 + j, y] for j in range(n + 1)]
                for j in range(n):
                    w_up = wu[x + j, y]
                    near = (
                        (faces[j] * rows[j] + faces[j + 1] * rows[j + 2])
                        + (w_prev[j] * v_prev[j] + w_next[j] * v_next[j])
                        + (pltpu.roll(w_up * v_here[j], 1, 1) + w_up * pltpu.roll(v_here[j], nz - 1, 1))
                    )
                    value = (rhs[x + j, y] + near) * rden[x + j, y]
                    if k == SWEEPS - 1:
                        out[x + j - lead, y - k] = value
                    else:
                        new[X + j, y] = value
            return carry

        lax.fori_loop(0, count // n, sweep, 0)
        old, new = new, old


def wave(diagonal, group, plan, fields, nz, strips, inflow, common, kept):
    levels = plan.levels
    going = [p for p in group if diagonal - p < STEPS]
    keepers = [p for p in going if p < levels - 1]
    old = [p for p in group if 0 < diagonal - p and p < levels - 1]
    emits = group[-1] in old
    core = (plan.core_x, plan.core_y, fields, nz)
    sources, where = [], {}
    for p in group:
        arrays, index = strips[p]
        if not (sources and sources[-1] is arrays[-1]):
            sources += list(arrays)
        where[p] = (len(sources) - 3, index)
    n_src = len(sources)
    extra = [] if inflow is None else [inflow]

    def kernel(*refs):
        refs = list(refs)
        take = lambda n: [refs.pop(0) for _ in range(n)]
        src = take(n_src)
        rate_ref, mask_ref, half_ref, loss_ref, mats_ref = take(5)
        old_refs = dict(zip(old, take(len(old))))
        in_refs = take(len(extra))
        state_refs = take(1) if going else []
        new_refs = dict(zip(keepers, take(len(keepers))))
        out_refs = take(1) if emits else []
        held = refs.pop(-1)
        u, c, _, va, vb = refs[:5]
        env = {"scratch": refs, "rate": rate_ref, "mask": mask_ref, "half_d": half_ref, "loss": loss_ref, "mats": mats_ref}
        if plan.closed:
            for x in (0, plan.wide_x - 1):
                for y in range(plan.wide_y):
                    u[x, y] = jnp.zeros((fields, nz), jnp.float32)
                    c[x, y] = half_ref[...]
                for y in range(plan.core_y):
                    va[x, y] = jnp.zeros((fields, nz), jnp.float32)
                    vb[x, y] = jnp.zeros((fields, nz), jnp.float32)
        for p in group:
            node = diagonal - p
            at, index = where[p]
            inflow_in = None if p == 0 or node == STEPS else (in_refs[0] if p == group[0] else held)
            inflow_out = None if p not in old else (out_refs[0] if p == group[-1] else held)
            level_pass(
                [r.at[index] for r in src[at : at + 3]], env, plan, node, inflow_in, inflow_out,
                old_refs.get(p), new_refs.get(p), state_refs[0].at[going.index(p)] if p in going else None,
            )

    vmem = pl.BlockSpec(memory_space=pltpu.VMEM)
    smem = pl.BlockSpec(memory_space=pltpu.SMEM)
    f32 = jnp.float32
    operands = sources + list(common) + [kept[p] for p in old] + extra
    in_specs = [vmem] * n_src + [vmem, smem, vmem, vmem, vmem] + [vmem] * (len(old) + len(extra))
    out_shape = [jax.ShapeDtypeStruct((len(going), plan.sub_x, plan.sub_y, fields, nz), f32)] if going else []
    out_shape += [jax.ShapeDtypeStruct(core, f32)] * (len(keepers) + emits)
    cells = core[0] * core[1] * fields * nz
    wide = (plan.wide_x, plan.wide_y, fields, nz)
    tall = (plan.wide_x,) + core[1:]
    chem = (2, 2) + core[1:]
    shapes = [wide, wide, chem, tall, tall, tall, core, core, core, core, core]
    results = list(pl.pallas_call(
        kernel,
        out_shape=out_shape,
        in_specs=in_specs,
        out_specs=[vmem] * len(out_shape),
        scratch_shapes=[pltpu.VMEM(s, f32) for s in shapes],
        compiler_params=pltpu.CompilerParams(vmem_limit_bytes=56 * 2**20),
        cost_estimate=pl.CostEstimate(flops=150 * cells * len(group), bytes_accessed=8 * cells * len(group), transcendentals=0),
        name="wave%d_%d" % (diagonal, group[0]),
    )(*operands))
    states = results.pop(0) if going else None
    return going, states, dict(zip(keepers, results)), results[-1] if emits else None


def inside_mask(plan):
    part, gx, gy = (lax.axis_index(a) for a in AXES)
    offsets = jnp.arange(max(plan.core_x, plan.core_y))
    cols = (gy * plan.parts_y + part % plan.parts_y) * plan.sub_y + offsets - RIM
    if plan.closed:
        rows = offsets
    else:
        half = part // plan.parts_y
        half = jnp.where(gx % 2 == 0, half, plan.parts_x - 1 - half)
        rows = (gx * plan.parts_x + half) * plan.sub_x + offsets - RIM
    row_ok = (rows >= 0) & (rows < plan.rows * plan.gx)
    col_ok = (cols >= 0) & (cols < plan.cols * plan.gy)
    return jnp.stack([row_ok, col_ok]).astype(jnp.float32)


def matrix_halves(x):
    high = lax.reduce_precision(x, 8, 7)
    return high, x - high


def gather_finals(finals, plan):
    part, gx = lax.axis_index("lvl"), lax.axis_index("gx")
    if not plan.closed:
        parts = lax.all_to_all(jnp.stack(finals), "lvl", 0, 0, tiled=True)
        parts = parts.reshape((plan.parts_x, plan.parts_y) + parts.shape[1:])
        parts = jnp.where(gx % 2 == 0, parts, parts[::-1])
        return jnp.transpose(parts, (0, 2, 1, 3, 4, 5)).reshape((plan.rows, plan.cols) + parts.shape[4:])
    whole = jnp.stack(finals)
    whole = lax.dynamic_slice_in_dim(whole, gx * plan.rows, plan.rows, axis=1)
    n = plan.parts_y
    group = part // n
    column = part % n
    blocks = [None] * n
    got = [lax.dynamic_index_in_dim(whole, part, 0, keepdims=False)]
    for r in range(1, n):
        pairs = [(p, p // n * n + (p % n + r) % n) for p in range(plan.levels)]
        theirs = lax.dynamic_index_in_dim(whole, group * n + (column + r) % n, 0, keepdims=False)
        got.append(lax.ppermute(theirs, "lvl", pairs))
    stack = jnp.stack(got)
    order = jnp.stack([lax.dynamic_index_in_dim(stack, (column - k) % n, 0, keepdims=False) for k in range(n)], axis=1)
    return order.reshape((plan.rows, plan.cols) + order.shape[3:])


def grouped(active):
    return [active[i : i + GROUP] for i in range(0, len(active), GROUP)]


def on_device(initial, rate_factor, diffusivity, loss_rate, quench, formation):
    fields, rows, cols, nz = initial.shape
    plan = Plan(rows, cols)
    levels = plan.levels

    started, rate = columns(jnp.transpose(initial, (1, 2, 0, 3)), rate_factor, plan)
    started = [x[None] for x in started]
    rate = jnp.concatenate(rate, axis=1)
    rate = rate[:, 1:-1] if plan.closed else rate[1:-1, 1:-1]
    mask = inside_mask(plan)

    reacting = (jnp.arange(fields) < REACT).astype(jnp.float32)
    half_d = jnp.broadcast_to(0.5 * diffusivity[:, None], (fields, nz))
    loss = jnp.broadcast_to((reacting * loss_rate)[:, None], (fields, nz))
    eye = jnp.eye(plan.core_y, dtype=jnp.float32)
    mats = []
    for matrix in ((reacting * loss_rate)[:, None] * quench, reacting[:, None] * formation):
        mats.append(jnp.concatenate([jnp.kron(eye, m) for m in matrix_halves(matrix)], axis=0))
    common = [rate, mask, half_d, loss, jnp.stack(mats).astype(jnp.bfloat16)]

    strips, kept, finals = {}, {}, {}
    for diagonal in range(levels + STEPS - 1):
        if diagonal < levels:
            strips[diagonal] = (started, 0)
        active = [p for p in sorted(strips) if diagonal - p < STEPS + (p < levels - 1)]
        inflow, fresh, held = None, {}, {}
        for group in grouped(active):
            going, states, keeps, inflow = wave(diagonal, group, plan, fields, nz, strips, inflow, common, kept)
            held.update(keeps)
            for i, p in enumerate(going):
                if diagonal - p + 1 == STEPS:
                    finals[p] = states[i]
            if going and not (diagonal - going[0] + 1 == STEPS and going[0] == levels - 1):
                arrays = exchange(states, plan)
                fresh.update({p: (arrays, i) for i, p in enumerate(going)})
        strips, kept = fresh, held
    tile = gather_finals([finals[p] for p in range(levels)], plan)
    return jnp.transpose(tile, (2, 0, 1, 3))[None]


def solution(mesh):
    in_specs = (P(None, "gx", "gy", None), P("gx", "gy", None), P(), P(), P(), P())
    out_specs = P("lvl", None, "gx", "gy", None)
    return jax.shard_map(
        on_device, mesh=mesh, in_specs=in_specs, out_specs=out_specs, check_vma=False
    )
```

```python
import functools

import jax
import jax.numpy as jnp
from jax import lax
from jax.experimental import pallas as pl
from jax.experimental.pallas import tpu as pltpu
from jax.sharding import PartitionSpec as P

REACT = 11
STEPS = 4
SWEEPS = 4
RIM = SWEEPS - 1
GROUP = 2
AXES = ("lvl", "gx", "gy")


class Plan:
    def __init__(self, rows, cols):
        self.levels, self.gx, self.gy = (lax.axis_size(a) for a in AXES)
        self.rows, self.cols = rows, cols
        self.closed = self.gx <= 2
        parts = self.levels
        if self.closed:
            self.parts_x, self.parts_y = 1, 1
            while parts % (2 * self.parts_y) == 0 and cols // (2 * self.parts_y) >= SWEEPS:
                self.parts_y *= 2
            self.sub_x, self.wide_x = rows * self.gx, rows * self.gx + 2
        else:
            self.parts_x = 1
            while self.parts_x * self.parts_x < parts:
                self.parts_x *= 2
            self.parts_y = parts // self.parts_x
            assert self.parts_x * self.parts_y == parts and rows % self.parts_x == 0
            self.sub_x, self.wide_x = rows // self.parts_x, rows // self.parts_x + 2 * SWEEPS
        assert cols % self.parts_y == 0
        self.sub_y = cols // self.parts_y
        assert min(self.sub_x, self.sub_y) >= SWEEPS
        self.wide_y = self.sub_y + 2 * SWEEPS
        self.core_x, self.core_y = self.wide_x - 2, self.wide_y - 2
        self.paired = self.closed and self.parts_y == 2 and self.sub_y == SWEEPS

    def spot(self, part, gx, gy):
        at_y = gy * self.parts_y + part % self.parts_y
        if self.closed:
            return gx, part // self.parts_y, at_y
        half = part // self.parts_y
        half = half if gx % 2 == 0 else self.parts_x - 1 - half
        return gx * self.parts_x + half, 0, at_y

    def devices(self):
        found = {}
        for part in range(self.levels):
            for gx in range(self.gx):
                for gy in range(self.gy):
                    found[self.spot(part, gx, gy)] = (part * self.gx + gx) * self.gy + gy
        return found

    def column(self, device):
        return device // (self.gx * self.gy) % self.parts_y

    def swaps(self, outside):
        return sorted(
            [(a, b) for a, b in self.shifts(0, 1) if self.column(a) == (1 if outside else 0)]
            + [(a, b) for a, b in self.shifts(0, -1) if self.column(a) == (0 if outside else 1)]
        )

    def shifts(self, dx, dy):
        found = self.devices()
        there = lambda s: (s[0] + dx, s[1], s[2] + dy)
        return [(d, found[there(s)]) for s, d in sorted(found.items()) if there(s) in found]


def columns(own, rate, plan):
    half = lax.axis_index("lvl") % plan.parts_y
    gx = lax.axis_index("gx")
    sub, nz = plan.sub_y, own.shape[-1]
    if plan.closed:
        def pack(x, r):
            return jnp.concatenate([x.reshape(-1, nz), r.reshape(-1, nz)], axis=0)

        def unpack(packed, x, r):
            return packed[: x.size // nz].reshape(x.shape), packed[x.size // nz :].reshape(r.shape)

        if plan.gx == 2:
            theirs = unpack(lax.ppermute(pack(own, rate), "gx", [(0, 1), (1, 0)]), own, rate)
            own, rate = (
                jnp.where(gx == 0, jnp.concatenate([a, b], axis=0), jnp.concatenate([b, a], axis=0))
                for a, b in zip((own, rate), theirs)
            )
        if plan.paired:
            low, high = ([x[:, :sub] for x in (own, rate)], [x[:, sub:] for x in (own, rate)])
            mine = [jnp.where(half == 0, a, b) for a, b in zip(low, high)]
            inner = [jnp.where(half == 0, b, a) for a, b in zip(low, high)]
            outer = unpack(lax.ppermute(pack(*mine), AXES, plan.swaps(True)), *mine)
            rates = jnp.where(half == 0, jnp.concatenate([outer[1], rate], axis=1), jnp.concatenate([rate, outer[1]], axis=1))
            return (inner[0], mine[0], outer[0]), rates
        both = jnp.concatenate([own, rate[:, :, None, :]], axis=2)
    else:
        both = jnp.concatenate([own, rate[:, :, None, :]], axis=2)
        at = lax.axis_index("lvl") // plan.parts_y
        at = jnp.where(gx % 2 == 0, at, plan.parts_x - 1 - at) * plan.sub_x
        both = lax.dynamic_slice_in_dim(both, at, plan.sub_x, axis=0)
    both = lax.dynamic_slice_in_dim(both, half * sub, sub, axis=1)
    strips = exchange(both[None], plan)
    return [x[0, :, :, :-1] for x in strips], jnp.concatenate([x[0, :, :, -1] for x in strips], axis=1)


def exchange(states, plan):
    if plan.paired:
        return lax.ppermute(states, AXES, plan.swaps(False)), states, lax.ppermute(states, AXES, plan.swaps(True))
    if not plan.closed:
        before = lax.ppermute(states[:, -SWEEPS:], AXES, plan.shifts(1, 0))
        after = lax.ppermute(states[:, :SWEEPS], AXES, plan.shifts(-1, 0))
        states = jnp.concatenate([before, states, after], axis=1)
    before = lax.ppermute(states[:, :, -SWEEPS:], AXES, plan.shifts(0, 1))
    after = lax.ppermute(states[:, :, :SWEEPS], AXES, plan.shifts(0, -1))
    return before, states, after


def halves(x):
    high = x.astype(jnp.bfloat16)
    return high, (x - high.astype(jnp.float32)).astype(jnp.bfloat16)


def product(matrix, x):
    dot = functools.partial(jnp.dot, preferred_element_type=jnp.float32)
    n = matrix.shape[0] // 2
    high, low = halves(x)
    first = dot(matrix, high)
    return first[:n] + (first[n:] + dot(matrix[:n], low))


def level_pass(strips, env, plan, node, inflow_in, inflow_out, kept_old, kept_new, out, fresh):
    u, c, chem, va, vb, wx, wy, wu, rhs, rden = env["scratch"]
    first = va
    if fresh is not None:
        first, wx, wy, wu, rhs, rden = fresh[:6]
    rate, mask, half_d, loss, mats = env["rate"], env["mask"], env["half_d"], env["loss"], env["mats"]
    fields, nz = u.shape[2:]
    rx, ry = plan.core_x, plan.core_y
    hd = half_d[...]
    base = 1 if plan.closed else 0

    def conduct(value):
        return hd + hd * (value * value)

    starts = [0, strips[0].shape[1], strips[0].shape[1] + strips[1].shape[1]]
    if plan.paired:
        side = env["side"][0]
        starts[0], starts[2] = (1 - side) * starts[2], side * starts[2]

    def widen(x, carry):
        for at, strip in zip(starts, strips):
            for y in range(strip.shape[1]):
                value = strip[x, y]
                u[x + base, at + y] = value
                c[x + base, at + y] = conduct(value)
        return carry

    lax.fori_loop(0, strips[0].shape[0], widen, 0)

    lane = lax.broadcasted_iota(jnp.int32, (fields, nz), 1)
    bottom, top = lane == 0, lane == nz - 1
    lr = loss[...]
    advance = node < STEPS

    def setup(x, k):
        X = x + 1
        u_here, u_next = u[X, 0], u[X, 1]
        c_here, c_next = c[X, 0], c[X, 1]
        wy_next = c_here + c_next
        for y in range(ry):
            Y = y + 1
            u_prev, u_here, u_next = u_here, u_next, u[X, Y + 1]
            c_here, c_next = c_next, c[X, Y + 1]
            wy_prev, wy_next = wy_next, c_here + c_next
            wx_prev = c_here + c[X - 1, Y]
            wx_next = c_here + c[X + 1, Y]
            below = jnp.where(bottom, 0.0, pltpu.roll(u_here, 1, 1))
            above = jnp.where(top, 0.0, pltpu.roll(u_here, nz - 1, 1))
            w_low = c_here + conduct(below)
            w_up = c_here + conduct(above)
            weights = ((wx_prev + wx_next) + (wy_prev + wy_next)) + (w_low + w_up)
            near = (
                (wx_prev * u[X - 1, Y] + wx_next * u[X + 1, Y])
                + (wy_prev * u_prev + wy_next * u_next)
                + (w_low * below + w_up * above)
            )
            factor = jnp.broadcast_to(rate[x, pl.ds(y, 1), :], (fields, nz))
            made = factor * chem[1, k, y]
            drop = factor * (lr + chem[0, k, y]) + weights
            if advance:
                source = u_here + inflow_in[x, y] if inflow_in is not None else u_here
            if inflow_out is not None or kept_new is not None:
                half_t = 0.5 * (near + made - drop * u_here)
            if inflow_out is not None:
                inflow_out[x, y] = kept_old[x, y] + (half_t - u_here)
            if kept_new is not None:
                kept_new[x, y] = half_t + source
            if advance:
                right = source + made
                inverse = (mask[0, x] * mask[1, y]) / (1.0 + drop)
                rhs[x, y] = right
                rden[x, y] = inverse
                wx[X, y] = wx_next
                wy[x, y] = wy_next
                wu[x, y] = jnp.where(top, 0.0, w_up)
                first[X, y] = (right + near) * inverse

    def rows_two(i, carry):
        value = jnp.concatenate([u[2 * i + 1 + k, 1 : 1 + ry].reshape(ry * fields, nz) for k in range(2)], axis=1)
        for j, result in enumerate((product(mats[0], value * value), product(mats[1], value))):
            for k in range(2):
                chem[j, k] = result[:, k * nz : (k + 1) * nz].reshape(ry, fields, nz)
        for k in range(2):
            setup(2 * i + k, k)
        return carry

    lax.fori_loop(0, rx // 2, rows_two, 0)
    if not advance:
        return
    if plan.closed:
        for y in range(ry):
            wx[0, y] = c[0, y + 1] + c[1, y + 1]
    sweeps(plan, first, va, vb, wx, wy, wu, rhs, rden, out)


def first_pass(env, plan, inflow, kept_new, out, fresh):
    va, vb, rhs = env["scratch"][3], env["scratch"][4], env["scratch"][8]
    first, wx, wy, wu, right, rden, kept = fresh

    def add(x, carry):
        for y in range(plan.core_y):
            more = inflow[x, y]
            rhs[x, y] = right[x, y] + more
            va[x + 1, y] = first[x + 1, y] + more * rden[x, y]
            if kept_new is not None:
                kept_new[x, y] = kept[x, y] + more
        return carry

    lax.fori_loop(0, plan.core_x, add, 0)
    sweeps(plan, va, va, vb, wx, wy, wu, rhs, rden, out)


def sweeps(plan, first, va, vb, wx, wy, wu, rhs, rden, out):
    nz = vb.shape[3]
    rx, ry = plan.core_x, plan.core_y
    shrink = 0 if plan.closed else 1
    old, new, spare = first, vb, va
    for k in range(1, SWEEPS):
        lead = k * shrink
        count = rx - 2 * lead
        n = 4 if count % 4 == 0 else 2

        def sweep(i, carry, k=k, old=old, new=new, lead=lead, n=n):
            x = lead + n * i
            X = x + 1
            v_here = [old[X + j, k - 1] for j in range(n)]
            v_next = [old[X + j, k] for j in range(n)]
            w_next = [wy[x + j, k - 1] for j in range(n)]
            for y in range(k, ry - k):
                v_prev, v_here, v_next = v_here, v_next, [old[X + j, y + 1] for j in range(n)]
                w_prev, w_next = w_next, [wy[x + j, y] for j in range(n)]
                rows = [old[X - 1, y]] + v_here + [old[X + n, y]]
                faces = [wx[X - 1 + j, y] for j in range(n + 1)]
                for j in range(n):
                    w_up = wu[x + j, y]
                    near = (
                        (faces[j] * rows[j] + faces[j + 1] * rows[j + 2])
                        + (w_prev[j] * v_prev[j] + w_next[j] * v_next[j])
                        + (pltpu.roll(w_up * v_here[j], 1, 1) + w_up * pltpu.roll(v_here[j], nz - 1, 1))
                    )
                    value = (rhs[x + j, y] + near) * rden[x + j, y]
                    if k == SWEEPS - 1:
                        out[x + j - lead, y - k] = value
                    else:
                        new[X + j, y] = value
            return carry

        lax.fori_loop(0, count // n, sweep, 0)
        old, new, spare = new, spare, new


def wave(diagonal, group, plan, fields, nz, strips, inflow, common, kept, cache):
    levels = plan.levels
    going = [p for p in group if diagonal - p < STEPS]
    keepers = [p for p in going if p < levels - 1]
    old = [p for p in group if 0 < diagonal - p and p < levels - 1]
    emits = group[-1] in old
    core = (plan.core_x, plan.core_y, fields, nz)
    sources, where = [], {}
    for p in group:
        if p == diagonal and p > 0:
            continue
        arrays, index = strips[p]
        if not (sources and sources[-1] is arrays[-1]):
            sources += list(arrays)
        where[p] = (len(sources) - 3, index)
    n_src = len(sources)
    extra = [] if inflow is None else [inflow]
    makes = diagonal == 0
    shared = list(cache) if diagonal > 0 and diagonal in group else []

    def kernel(*refs):
        refs = list(refs)
        take = lambda n: [refs.pop(0) for _ in range(n)]
        src = take(n_src)
        rate_ref, mask_ref, side_ref, half_ref, loss_ref, mats_ref = take(6)
        old_refs = dict(zip(old, take(len(old))))
        in_refs = take(len(extra))
        shared_refs = take(len(shared))
        state_refs = take(1) if going else []
        new_refs = dict(zip(keepers, take(len(keepers))))
        out_refs = take(1) if emits else []
        made_refs = take(6) if makes else []
        held = refs.pop(-1)
        u, c, _, va, vb = refs[:5]
        env = {"scratch": refs, "rate": rate_ref, "mask": mask_ref, "side": side_ref, "half_d": half_ref, "loss": loss_ref, "mats": mats_ref}
        if plan.closed:
            for x in (0, plan.wide_x - 1):
                for y in range(plan.wide_y):
                    u[x, y] = jnp.zeros((fields, nz), jnp.float32)
                    c[x, y] = half_ref[...]
                for y in range(plan.core_y):
                    va[x, y] = jnp.zeros((fields, nz), jnp.float32)
                    vb[x, y] = jnp.zeros((fields, nz), jnp.float32)
                    if makes:
                        made_refs[0][x, y] = jnp.zeros((fields, nz), jnp.float32)
        for p in group:
            node = diagonal - p
            inflow_in = None if p == 0 or node == STEPS else (in_refs[0] if p == group[0] else held)
            inflow_out = None if p not in old else (out_refs[0] if p == group[-1] else held)
            out = state_refs[0].at[going.index(p)] if p in going else None
            if node == 0 and p > 0:
                first_pass(env, plan, inflow_in, new_refs.get(p), out, shared_refs)
                continue
            at, index = where[p]
            level_pass(
                [r.at[index] for r in src[at : at + 3]], env, plan, node, inflow_in, inflow_out,
                old_refs.get(p), new_refs.get(p), out, made_refs if makes else None,
            )

    vmem = pl.BlockSpec(memory_space=pltpu.VMEM)
    smem = pl.BlockSpec(memory_space=pltpu.SMEM)
    f32 = jnp.float32
    operands = sources + list(common) + [kept[p] for p in old] + extra + shared
    in_specs = [vmem] * n_src + [vmem, smem, smem, vmem, vmem, vmem] + [vmem] * (len(old) + len(extra) + len(shared))
    out_shape = [jax.ShapeDtypeStruct((len(going), plan.sub_x, plan.sub_y, fields, nz), f32)] if going else []
    out_shape += [jax.ShapeDtypeStruct(core, f32)] * (len(keepers) + emits)
    cells = core[0] * core[1] * fields * nz
    wide = (plan.wide_x, plan.wide_y, fields, nz)
    tall = (plan.wide_x,) + core[1:]
    chem = (2, 2) + core[1:]
    if makes:
        out_shape += [jax.ShapeDtypeStruct(shape, f32) for shape in (tall, tall, core, core, core, core)]
    shapes = [wide, wide, chem, tall, tall, tall, core, core, core, core, core]
    results = list(pl.pallas_call(
        kernel,
        out_shape=out_shape,
        in_specs=in_specs,
        out_specs=[vmem] * len(out_shape),
        scratch_shapes=[pltpu.VMEM(s, f32) for s in shapes],
        compiler_params=pltpu.CompilerParams(vmem_limit_bytes=30 * 2**20),
        cost_estimate=pl.CostEstimate(flops=150 * cells * len(group), bytes_accessed=8 * cells * len(group), transcendentals=0),
        name="wave%d_%d" % (diagonal, group[0]),
    )(*operands))
    states = results.pop(0) if going else None
    held = dict(zip(keepers, results))
    if makes:
        cache.extend(results[-6:] + [held[0]])
    return going, states, held, results[-1] if emits else None


def inside_mask(plan):
    part, gx, gy = (lax.axis_index(a) for a in AXES)
    offsets = jnp.arange(max(plan.core_x, plan.core_y))
    cols = (gy * plan.parts_y + part % plan.parts_y) * plan.sub_y + offsets - RIM
    if plan.closed:
        rows = offsets
    else:
        half = part // plan.parts_y
        half = jnp.where(gx % 2 == 0, half, plan.parts_x - 1 - half)
        rows = (gx * plan.parts_x + half) * plan.sub_x + offsets - RIM
    row_ok = (rows >= 0) & (rows < plan.rows * plan.gx)
    col_ok = (cols >= 0) & (cols < plan.cols * plan.gy)
    return jnp.stack([row_ok, col_ok]).astype(jnp.float32)


def matrix_halves(x):
    high = lax.reduce_precision(x, 8, 7)
    return high, x - high


def gather_finals(finals, plan):
    part, gx = lax.axis_index("lvl"), lax.axis_index("gx")
    if not plan.closed:
        parts = lax.all_to_all(jnp.stack(finals), "lvl", 0, 0, tiled=True)
        parts = parts.reshape((plan.parts_x, plan.parts_y) + parts.shape[1:])
        parts = jnp.where(gx % 2 == 0, parts, parts[::-1])
        return jnp.transpose(parts, (0, 2, 1, 3, 4, 5)).reshape((plan.rows, plan.cols) + parts.shape[4:])
    whole = jnp.stack(finals)
    whole = lax.dynamic_slice_in_dim(whole, gx * plan.rows, plan.rows, axis=1)
    n = plan.parts_y
    group = part // n
    column = part % n
    blocks = [None] * n
    got = [lax.dynamic_index_in_dim(whole, part, 0, keepdims=False)]
    for r in range(1, n):
        pairs = [(p, p // n * n + (p % n + r) % n) for p in range(plan.levels)]
        theirs = lax.dynamic_index_in_dim(whole, group * n + (column + r) % n, 0, keepdims=False)
        got.append(lax.ppermute(theirs, "lvl", pairs))
    stack = jnp.stack(got)
    order = jnp.stack([lax.dynamic_index_in_dim(stack, (column - k) % n, 0, keepdims=False) for k in range(n)], axis=1)
    return order.reshape((plan.rows, plan.cols) + order.shape[3:])


def grouped(active):
    size = 1 if len(active) == 2 and active[0] == 0 else GROUP
    return [active[i : i + size] for i in range(0, len(active), size)]


def on_device(initial, rate_factor, diffusivity, loss_rate, quench, formation):
    fields, rows, cols, nz = initial.shape
    plan = Plan(rows, cols)
    levels = plan.levels

    started, rate = columns(jnp.transpose(initial, (1, 2, 0, 3)), rate_factor, plan)
    started = [x[None] for x in started]
    rate = rate[:, 1:-1] if plan.closed else rate[1:-1, 1:-1]
    mask = inside_mask(plan)

    reacting = (jnp.arange(fields) < REACT).astype(jnp.float32)
    half_d = jnp.broadcast_to(0.5 * diffusivity[:, None], (fields, nz))
    loss = jnp.broadcast_to((reacting * loss_rate)[:, None], (fields, nz))
    eye = jnp.eye(plan.core_y, dtype=jnp.float32)
    mats = []
    for matrix in ((reacting * loss_rate)[:, None] * quench, reacting[:, None] * formation):
        mats.append(jnp.concatenate([jnp.kron(eye, m) for m in matrix_halves(matrix)], axis=0))
    side = (lax.axis_index("lvl") % plan.parts_y).astype(jnp.int32)[None]
    common = [rate, mask, side, half_d, loss, jnp.stack(mats).astype(jnp.bfloat16)]

    strips, kept, finals, cache = {}, {}, {}, []
    for diagonal in range(levels + STEPS - 1):
        if diagonal < levels:
            strips[diagonal] = (started, 0) if diagonal == 0 else None
        active = [p for p in sorted(strips) if diagonal - p < STEPS + (p < levels - 1)]
        inflow, fresh, held = None, {}, {}
        for group in grouped(active):
            going, states, keeps, inflow = wave(diagonal, group, plan, fields, nz, strips, inflow, common, kept, cache)
            held.update(keeps)
            for i, p in enumerate(going):
                if diagonal - p + 1 == STEPS:
                    finals[p] = states[i]
            if going and not (diagonal - going[0] + 1 == STEPS and going[0] == levels - 1):
                arrays = exchange(states, plan)
                fresh.update({p: (arrays, i) for i, p in enumerate(going)})
        strips, kept = fresh, held
    tile = gather_finals([finals[p] for p in range(levels)], plan)
    return jnp.transpose(tile, (2, 0, 1, 3))[None]


def solution(mesh):
    in_specs = (P(None, "gx", "gy", None), P("gx", "gy", None), P(), P(), P(), P())
    out_specs = P("lvl", None, "gx", "gy", None)
    return jax.shard_map(
        on_device, mesh=mesh, in_specs=in_specs, out_specs=out_specs, check_vma=False
    )
```

```python
import functools

import jax
import jax.numpy as jnp
from jax import lax
from jax.experimental import pallas as pl
from jax.experimental.pallas import tpu as pltpu
from jax.sharding import PartitionSpec as P

REACT = 11
STEPS = 4
SWEEPS = 4
RIM = SWEEPS - 1
AXES = ("lvl", "gx", "gy")


class Plan:
    def __init__(self, rows, cols):
        self.levels, self.gx, self.gy = (lax.axis_size(a) for a in AXES)
        self.rows, self.cols = rows, cols
        self.closed = self.gx <= 2
        parts = self.levels
        if self.closed:
            self.parts_x, self.parts_y = 1, 1
            while parts % (2 * self.parts_y) == 0 and cols // (2 * self.parts_y) >= SWEEPS:
                self.parts_y *= 2
            self.sub_x, self.wide_x = rows * self.gx, rows * self.gx + 2
        else:
            self.parts_x = 1
            while self.parts_x * self.parts_x < parts:
                self.parts_x *= 2
            self.parts_y = parts // self.parts_x
            assert self.parts_x * self.parts_y == parts and rows % self.parts_x == 0
            self.sub_x, self.wide_x = rows // self.parts_x, rows // self.parts_x + 2 * SWEEPS
        assert cols % self.parts_y == 0
        self.sub_y = cols // self.parts_y
        assert min(self.sub_x, self.sub_y) >= SWEEPS
        self.wide_y = self.sub_y + 2 * SWEEPS
        self.core_x, self.core_y = self.wide_x - 2, self.wide_y - 2
        self.paired = self.closed and self.parts_y == 2 and self.sub_y == SWEEPS

    def spot(self, part, gx, gy):
        at_y = gy * self.parts_y + part % self.parts_y
        if self.closed:
            return gx, part // self.parts_y, at_y
        half = part // self.parts_y
        half = half if gx % 2 == 0 else self.parts_x - 1 - half
        return gx * self.parts_x + half, 0, at_y

    def devices(self):
        found = {}
        for part in range(self.levels):
            for gx in range(self.gx):
                for gy in range(self.gy):
                    found[self.spot(part, gx, gy)] = (part * self.gx + gx) * self.gy + gy
        return found

    def column(self, device):
        return device // (self.gx * self.gy) % self.parts_y

    def swaps(self, outside):
        return sorted(
            [(a, b) for a, b in self.shifts(0, 1) if self.column(a) == (1 if outside else 0)]
            + [(a, b) for a, b in self.shifts(0, -1) if self.column(a) == (0 if outside else 1)]
        )

    def shifts(self, dx, dy):
        found = self.devices()
        there = lambda s: (s[0] + dx, s[1], s[2] + dy)
        return [(d, found[there(s)]) for s, d in sorted(found.items()) if there(s) in found]


def columns(own, rate, plan):
    half = lax.axis_index("lvl") % plan.parts_y
    gx = lax.axis_index("gx")
    sub, nz = plan.sub_y, own.shape[-1]
    if plan.closed:
        def pack(x, r):
            return jnp.concatenate([x.reshape(-1, nz), r.reshape(-1, nz)], axis=0)

        def unpack(packed, x, r):
            return packed[: x.size // nz].reshape(x.shape), packed[x.size // nz :].reshape(r.shape)

        if plan.gx == 2:
            theirs = unpack(lax.ppermute(pack(own, rate), "gx", [(0, 1), (1, 0)]), own, rate)
            own, rate = (
                jnp.where(gx == 0, jnp.concatenate([a, b], axis=0), jnp.concatenate([b, a], axis=0))
                for a, b in zip((own, rate), theirs)
            )
        if plan.paired:
            low, high = ([x[:, :sub] for x in (own, rate)], [x[:, sub:] for x in (own, rate)])
            mine = [jnp.where(half == 0, a, b) for a, b in zip(low, high)]
            inner = [jnp.where(half == 0, b, a) for a, b in zip(low, high)]
            outer = unpack(lax.ppermute(pack(*mine), AXES, plan.swaps(True)), *mine)
            rates = jnp.where(half == 0, jnp.concatenate([outer[1], rate], axis=1), jnp.concatenate([rate, outer[1]], axis=1))
            return (inner[0], mine[0], outer[0]), rates
        both = jnp.concatenate([own, rate[:, :, None, :]], axis=2)
    else:
        both = jnp.concatenate([own, rate[:, :, None, :]], axis=2)
        at = lax.axis_index("lvl") // plan.parts_y
        at = jnp.where(gx % 2 == 0, at, plan.parts_x - 1 - at) * plan.sub_x
        both = lax.dynamic_slice_in_dim(both, at, plan.sub_x, axis=0)
    both = lax.dynamic_slice_in_dim(both, half * sub, sub, axis=1)
    strips = exchange(both[None], plan)
    return [x[0, :, :, :-1] for x in strips], jnp.concatenate([x[0, :, :, -1] for x in strips], axis=1)


def exchange(states, plan):
    if plan.paired:
        return lax.ppermute(states, AXES, plan.swaps(False)), states, lax.ppermute(states, AXES, plan.swaps(True))
    if not plan.closed:
        before = lax.ppermute(states[:, -SWEEPS:], AXES, plan.shifts(1, 0))
        after = lax.ppermute(states[:, :SWEEPS], AXES, plan.shifts(-1, 0))
        states = jnp.concatenate([before, states, after], axis=1)
    before = lax.ppermute(states[:, :, -SWEEPS:], AXES, plan.shifts(0, 1))
    after = lax.ppermute(states[:, :, :SWEEPS], AXES, plan.shifts(0, -1))
    return before, states, after


def halves(x):
    high = x.astype(jnp.bfloat16)
    return high, (x - high.astype(jnp.float32)).astype(jnp.bfloat16)


def product(matrix, x):
    dot = functools.partial(jnp.dot, preferred_element_type=jnp.float32)
    n = matrix.shape[0] // 2
    high, low = halves(x)
    first = dot(matrix, high)
    return first[:n] + (first[n:] + dot(matrix[:n], low))


def level_pass(strips, env, plan, node, inflow_in, inflow_out, kept_old, kept_new, out, fresh):
    u, c, chem, va, vb, wx, wy, wu, rhs, rden = env["scratch"]
    first = va
    if fresh is not None:
        first, wx, wy, wu, rhs, rden = fresh[:6]
    rate, mask, half_d, loss, mats = env["rate"], env["mask"], env["half_d"], env["loss"], env["mats"]
    fields, nz = u.shape[2:]
    rx, ry = plan.core_x, plan.core_y
    hd = half_d[...]
    base = 1 if plan.closed else 0

    def conduct(value):
        return hd + hd * (value * value)

    starts = [0, strips[0].shape[1], strips[0].shape[1] + strips[1].shape[1]]
    if plan.paired:
        side = env["side"][0]
        starts[0], starts[2] = (1 - side) * starts[2], side * starts[2]

    def widen(x, carry):
        for at, strip in zip(starts, strips):
            for y in range(strip.shape[1]):
                value = strip[x, y]
                u[x + base, at + y] = value
                c[x + base, at + y] = conduct(value)
        return carry

    lax.fori_loop(0, strips[0].shape[0], widen, 0)

    lane = lax.broadcasted_iota(jnp.int32, (fields, nz), 1)
    bottom, top = lane == 0, lane == nz - 1
    lr = loss[...]
    advance = node < STEPS

    def setup(x, k):
        X = x + 1
        u_here, u_next = u[X, 0], u[X, 1]
        c_here, c_next = c[X, 0], c[X, 1]
        wy_next = c_here + c_next
        for y in range(ry):
            Y = y + 1
            u_prev, u_here, u_next = u_here, u_next, u[X, Y + 1]
            c_here, c_next = c_next, c[X, Y + 1]
            wy_prev, wy_next = wy_next, c_here + c_next
            wx_prev = c_here + c[X - 1, Y]
            wx_next = c_here + c[X + 1, Y]
            below = jnp.where(bottom, 0.0, pltpu.roll(u_here, 1, 1))
            above = jnp.where(top, 0.0, pltpu.roll(u_here, nz - 1, 1))
            w_low = c_here + conduct(below)
            w_up = c_here + conduct(above)
            weights = ((wx_prev + wx_next) + (wy_prev + wy_next)) + (w_low + w_up)
            near = (
                (wx_prev * u[X - 1, Y] + wx_next * u[X + 1, Y])
                + (wy_prev * u_prev + wy_next * u_next)
                + (w_low * below + w_up * above)
            )
            factor = jnp.broadcast_to(rate[x, pl.ds(y, 1), :], (fields, nz))
            made = factor * chem[1, k, y]
            drop = factor * (lr + chem[0, k, y]) + weights
            if advance:
                source = u_here + inflow_in[x, y] if inflow_in is not None else u_here
            if inflow_out is not None or kept_new is not None:
                half_t = 0.5 * (near + made - drop * u_here)
            if inflow_out is not None:
                inflow_out[x, y] = kept_old[x, y] + (half_t - u_here)
            if kept_new is not None:
                kept_new[x, y] = half_t + source
            if advance:
                right = source + made
                inverse = (mask[0, x] * mask[1, y]) / (1.0 + drop)
                rhs[x, y] = right
                rden[x, y] = inverse
                wx[X, y] = wx_next
                wy[x, y] = wy_next
                wu[x, y] = jnp.where(top, 0.0, w_up)
                first[X, y] = (right + near) * inverse

    def rows_two(i, carry):
        value = jnp.concatenate([u[2 * i + 1 + k, 1 : 1 + ry].reshape(ry * fields, nz) for k in range(2)], axis=1)
        for j, result in enumerate((product(mats[0], value * value), product(mats[1], value))):
            for k in range(2):
                chem[j, k] = result[:, k * nz : (k + 1) * nz].reshape(ry, fields, nz)
        for k in range(2):
            setup(2 * i + k, k)
        return carry

    lax.fori_loop(0, rx // 2, rows_two, 0)
    if not advance:
        return
    if plan.closed:
        for y in range(ry):
            wx[0, y] = c[0, y + 1] + c[1, y + 1]
    sweeps(plan, first, va, vb, wx, wy, wu, rhs, rden, out)


def first_pass(env, plan, inflow, kept_new, out, fresh):
    va, vb, rhs = env["scratch"][3], env["scratch"][4], env["scratch"][8]
    first, wx, wy, wu, right, rden, kept = fresh

    def add(x, carry):
        for y in range(plan.core_y):
            more = inflow[x, y]
            rhs[x, y] = right[x, y] + more
            va[x + 1, y] = first[x + 1, y] + more * rden[x, y]
            if kept_new is not None:
                kept_new[x, y] = kept[x, y] + more
        return carry

    lax.fori_loop(0, plan.core_x, add, 0)
    sweeps(plan, va, va, vb, wx, wy, wu, rhs, rden, out)


def sweeps(plan, first, va, vb, wx, wy, wu, rhs, rden, out):
    nz = vb.shape[3]
    rx, ry = plan.core_x, plan.core_y
    shrink = 0 if plan.closed else 1
    old, new, spare = first, vb, va
    for k in range(1, SWEEPS):
        lead = k * shrink
        count = rx - 2 * lead
        n = 4 if count % 4 == 0 else 2

        def sweep(i, carry, k=k, old=old, new=new, lead=lead, n=n):
            x = lead + n * i
            X = x + 1
            v_here = [old[X + j, k - 1] for j in range(n)]
            v_next = [old[X + j, k] for j in range(n)]
            w_next = [wy[x + j, k - 1] for j in range(n)]
            for y in range(k, ry - k):
                v_prev, v_here, v_next = v_here, v_next, [old[X + j, y + 1] for j in range(n)]
                w_prev, w_next = w_next, [wy[x + j, y] for j in range(n)]
                rows = [old[X - 1, y]] + v_here + [old[X + n, y]]
                faces = [wx[X - 1 + j, y] for j in range(n + 1)]
                for j in range(n):
                    w_up = wu[x + j, y]
                    near = (
                        (faces[j] * rows[j] + faces[j + 1] * rows[j + 2])
                        + (w_prev[j] * v_prev[j] + w_next[j] * v_next[j])
                        + (pltpu.roll(w_up * v_here[j], 1, 1) + w_up * pltpu.roll(v_here[j], nz - 1, 1))
                    )
                    value = (rhs[x + j, y] + near) * rden[x + j, y]
                    if k == SWEEPS - 1:
                        out[x + j - lead, y - k] = value
                    else:
                        new[X + j, y] = value
            return carry

        lax.fori_loop(0, count // n, sweep, 0)
        old, new, spare = new, spare, new


def wave(diagonal, group, plan, fields, nz, strips, inflow, common, kept, cache):
    levels = plan.levels
    going = [p for p in group if diagonal - p < STEPS]
    keepers = [p for p in going if p < levels - 1]
    old = [p for p in group if 0 < diagonal - p and p < levels - 1]
    emits = group[-1] in old
    core = (plan.core_x, plan.core_y, fields, nz)
    sources, where = [], {}
    for p in group:
        if p == diagonal and p > 0:
            continue
        arrays, index = strips[p]
        if not (sources and sources[-1] is arrays[-1]):
            sources += list(arrays)
        where[p] = (len(sources) - 3, index)
    n_src = len(sources)
    extra = [] if inflow is None else [inflow]
    makes = diagonal == 0
    shared = list(cache) if diagonal > 0 and diagonal in group else []

    def kernel(*refs):
        refs = list(refs)
        take = lambda n: [refs.pop(0) for _ in range(n)]
        src = take(n_src)
        rate_ref, mask_ref, side_ref, half_ref, loss_ref, mats_ref = take(6)
        old_refs = dict(zip(old, take(len(old))))
        in_refs = take(len(extra))
        shared_refs = take(len(shared))
        state_refs = take(1) if going else []
        new_refs = dict(zip(keepers, take(len(keepers))))
        out_refs = take(1) if emits else []
        made_refs = take(6) if makes else []
        held = refs.pop(-1)
        u, c, _, va, vb = refs[:5]
        env = {"scratch": refs, "rate": rate_ref, "mask": mask_ref, "side": side_ref, "half_d": half_ref, "loss": loss_ref, "mats": mats_ref}
        if plan.closed:
            for x in (0, plan.wide_x - 1):
                for y in range(plan.wide_y):
                    u[x, y] = jnp.zeros((fields, nz), jnp.float32)
                    c[x, y] = half_ref[...]
                for y in range(plan.core_y):
                    va[x, y] = jnp.zeros((fields, nz), jnp.float32)
                    vb[x, y] = jnp.zeros((fields, nz), jnp.float32)
                    if makes:
                        made_refs[0][x, y] = jnp.zeros((fields, nz), jnp.float32)
        for p in group:
            node = diagonal - p
            inflow_in = None if p == 0 or node == STEPS else (in_refs[0] if p == group[0] else held)
            inflow_out = None if p not in old else (out_refs[0] if p == group[-1] else held)
            out = state_refs[0].at[going.index(p)] if p in going else None
            if node == 0 and p > 0:
                first_pass(env, plan, inflow_in, new_refs.get(p), out, shared_refs)
                continue
            at, index = where[p]
            level_pass(
                [r.at[index] for r in src[at : at + 3]], env, plan, node, inflow_in, inflow_out,
                old_refs.get(p), new_refs.get(p), out, made_refs if makes else None,
            )

    vmem = pl.BlockSpec(memory_space=pltpu.VMEM)
    smem = pl.BlockSpec(memory_space=pltpu.SMEM)
    f32 = jnp.float32
    operands = sources + list(common) + [kept[p] for p in old] + extra + shared
    in_specs = [vmem] * n_src + [vmem, smem, smem, vmem, vmem, vmem] + [vmem] * (len(old) + len(extra) + len(shared))
    out_shape = [jax.ShapeDtypeStruct((len(going), plan.sub_x, plan.sub_y, fields, nz), f32)] if going else []
    out_shape += [jax.ShapeDtypeStruct(core, f32)] * (len(keepers) + emits)
    cells = core[0] * core[1] * fields * nz
    wide = (plan.wide_x, plan.wide_y, fields, nz)
    tall = (plan.wide_x,) + core[1:]
    chem = (2, 2) + core[1:]
    if makes:
        out_shape += [jax.ShapeDtypeStruct(shape, f32) for shape in (tall, tall, core, core, core, core)]
    shapes = [wide, wide, chem, tall, tall, tall, core, core, core, core, core]
    results = list(pl.pallas_call(
        kernel,
        out_shape=out_shape,
        in_specs=in_specs,
        out_specs=[vmem] * len(out_shape),
        scratch_shapes=[pltpu.VMEM(s, f32) for s in shapes],
        compiler_params=pltpu.CompilerParams(vmem_limit_bytes=30 * 2**20),
        cost_estimate=pl.CostEstimate(flops=150 * cells * len(group), bytes_accessed=8 * cells * len(group), transcendentals=0),
        name="wave%d_%d" % (diagonal, group[0]),
    )(*operands))
    states = results.pop(0) if going else None
    held = dict(zip(keepers, results))
    if makes:
        cache.extend(results[-6:] + [held[0]])
    return going, states, held, results[-1] if emits else None


def inside_mask(plan):
    part, gx, gy = (lax.axis_index(a) for a in AXES)
    offsets = jnp.arange(max(plan.core_x, plan.core_y))
    cols = (gy * plan.parts_y + part % plan.parts_y) * plan.sub_y + offsets - RIM
    if plan.closed:
        rows = offsets
    else:
        half = part // plan.parts_y
        half = jnp.where(gx % 2 == 0, half, plan.parts_x - 1 - half)
        rows = (gx * plan.parts_x + half) * plan.sub_x + offsets - RIM
    row_ok = (rows >= 0) & (rows < plan.rows * plan.gx)
    col_ok = (cols >= 0) & (cols < plan.cols * plan.gy)
    return jnp.stack([row_ok, col_ok]).astype(jnp.float32)


def matrix_halves(x):
    high = lax.reduce_precision(x, 8, 7)
    return high, x - high


def gather_finals(finals, plan):
    part, gx = lax.axis_index("lvl"), lax.axis_index("gx")
    if not plan.closed:
        parts = lax.all_to_all(jnp.stack(finals), "lvl", 0, 0, tiled=True)
        parts = parts.reshape((plan.parts_x, plan.parts_y) + parts.shape[1:])
        parts = jnp.where(gx % 2 == 0, parts, parts[::-1])
        return jnp.transpose(parts, (0, 2, 1, 3, 4, 5)).reshape((plan.rows, plan.cols) + parts.shape[4:])
    whole = jnp.stack(finals)
    whole = lax.dynamic_slice_in_dim(whole, gx * plan.rows, plan.rows, axis=1)
    n = plan.parts_y
    group = part // n
    column = part % n
    blocks = [None] * n
    got = [lax.dynamic_index_in_dim(whole, part, 0, keepdims=False)]
    for r in range(1, n):
        pairs = [(p, p // n * n + (p % n + r) % n) for p in range(plan.levels)]
        theirs = lax.dynamic_index_in_dim(whole, group * n + (column + r) % n, 0, keepdims=False)
        got.append(lax.ppermute(theirs, "lvl", pairs))
    stack = jnp.stack(got)
    order = jnp.stack([lax.dynamic_index_in_dim(stack, (column - k) % n, 0, keepdims=False) for k in range(n)], axis=1)
    return order.reshape((plan.rows, plan.cols) + order.shape[3:])


def grouped(diagonal, active):
    groups = [[p] for p in active]
    if diagonal - active[0] == STEPS and len(groups) > 2:
        groups[:2] = [groups[0] + groups[1]]
    return groups


def on_device(initial, rate_factor, diffusivity, loss_rate, quench, formation):
    fields, rows, cols, nz = initial.shape
    plan = Plan(rows, cols)
    levels = plan.levels

    started, rate = columns(jnp.transpose(initial, (1, 2, 0, 3)), rate_factor, plan)
    started = [x[None] for x in started]
    rate = rate[:, 1:-1] if plan.closed else rate[1:-1, 1:-1]
    mask = inside_mask(plan)

    reacting = (jnp.arange(fields) < REACT).astype(jnp.float32)
    half_d = jnp.broadcast_to(0.5 * diffusivity[:, None], (fields, nz))
    loss = jnp.broadcast_to((reacting * loss_rate)[:, None], (fields, nz))
    eye = jnp.eye(plan.core_y, dtype=jnp.float32)
    mats = []
    for matrix in ((reacting * loss_rate)[:, None] * quench, reacting[:, None] * formation):
        mats.append(jnp.concatenate([jnp.kron(eye, m) for m in matrix_halves(matrix)], axis=0))
    side = (lax.axis_index("lvl") % plan.parts_y).astype(jnp.int32)[None]
    common = [rate, mask, side, half_d, loss, jnp.stack(mats).astype(jnp.bfloat16)]

    strips, kept, finals, cache = {}, {}, {}, []
    for diagonal in range(levels + STEPS - 1):
        if diagonal < levels:
            strips[diagonal] = (started, 0) if diagonal == 0 else None
        active = [p for p in sorted(strips) if diagonal - p < STEPS + (p < levels - 1)]
        inflow, fresh, held = None, {}, {}
        for group in grouped(diagonal, active):
            going, states, keeps, inflow = wave(diagonal, group, plan, fields, nz, strips, inflow, common, kept, cache)
            held.update(keeps)
            for i, p in enumerate(going):
                if diagonal - p + 1 == STEPS:
                    finals[p] = states[i]
            if going and not (diagonal - going[0] + 1 == STEPS and going[0] == levels - 1):
                arrays = exchange(states, plan)
                fresh.update({p: (arrays, i) for i, p in enumerate(going)})
        strips, kept = fresh, held
    tile = gather_finals([finals[p] for p in range(levels)], plan)
    return jnp.transpose(tile, (2, 0, 1, 3))[None]


def solution(mesh):
    in_specs = (P(None, "gx", "gy", None), P("gx", "gy", None), P(), P(), P(), P())
    out_specs = P("lvl", None, "gx", "gy", None)
    return jax.shard_map(
        on_device, mesh=mesh, in_specs=in_specs, out_specs=out_specs, check_vma=False
    )
```

```python
import functools

import jax
import jax.numpy as jnp
from jax import lax
from jax.experimental import pallas as pl
from jax.experimental.pallas import tpu as pltpu
from jax.sharding import PartitionSpec as P

REACT = 11
STEPS = 4
SWEEPS = 4
RIM = SWEEPS - 1
BLOCK = 4
AXES = ("lvl", "gx", "gy")


class Plan:
    def __init__(self, rows, cols):
        self.levels, self.gx, self.gy = (lax.axis_size(a) for a in AXES)
        self.rows, self.cols = rows, cols
        self.closed = self.gx <= 2
        parts = self.levels
        if self.closed:
            self.parts_x, self.parts_y = 1, 1
            while parts % (2 * self.parts_y) == 0 and cols // (2 * self.parts_y) >= SWEEPS:
                self.parts_y *= 2
            self.sub_x, self.wide_x = rows * self.gx, rows * self.gx + 2
        else:
            self.parts_x = 1
            while self.parts_x * self.parts_x < parts:
                self.parts_x *= 2
            self.parts_y = parts // self.parts_x
            assert self.parts_x * self.parts_y == parts and rows % self.parts_x == 0
            self.sub_x, self.wide_x = rows // self.parts_x, rows // self.parts_x + 2 * SWEEPS
        assert cols % self.parts_y == 0
        self.sub_y = cols // self.parts_y
        assert min(self.sub_x, self.sub_y) >= SWEEPS
        self.wide_y = self.sub_y + 2 * SWEEPS
        self.core_x, self.core_y = self.wide_x - 2, self.wide_y - 2
        self.paired = self.closed and self.parts_y == 2 and self.sub_y == SWEEPS

    def spot(self, part, gx, gy):
        at_y = gy * self.parts_y + part % self.parts_y
        if self.closed:
            return gx, part // self.parts_y, at_y
        half = part // self.parts_y
        half = half if gx % 2 == 0 else self.parts_x - 1 - half
        return gx * self.parts_x + half, 0, at_y

    def devices(self):
        found = {}
        for part in range(self.levels):
            for gx in range(self.gx):
                for gy in range(self.gy):
                    found[self.spot(part, gx, gy)] = (part * self.gx + gx) * self.gy + gy
        return found

    def column(self, device):
        return device // (self.gx * self.gy) % self.parts_y

    def swaps(self, outside):
        return sorted(
            [(a, b) for a, b in self.shifts(0, 1) if self.column(a) == (1 if outside else 0)]
            + [(a, b) for a, b in self.shifts(0, -1) if self.column(a) == (0 if outside else 1)]
        )

    def shifts(self, dx, dy):
        found = self.devices()
        there = lambda s: (s[0] + dx, s[1], s[2] + dy)
        return [(d, found[there(s)]) for s, d in sorted(found.items()) if there(s) in found]


def columns(own, rate, plan):
    half = lax.axis_index("lvl") % plan.parts_y
    gx = lax.axis_index("gx")
    sub, nz = plan.sub_y, own.shape[-1]
    if plan.closed:
        def pack(x, r):
            return jnp.concatenate([x.reshape(-1, nz), r.reshape(-1, nz)], axis=0)

        def unpack(packed, x, r):
            return packed[: x.size // nz].reshape(x.shape), packed[x.size // nz :].reshape(r.shape)

        if plan.gx == 2:
            theirs = unpack(lax.ppermute(pack(own, rate), "gx", [(0, 1), (1, 0)]), own, rate)
            own, rate = (
                jnp.where(gx == 0, jnp.concatenate([a, b], axis=0), jnp.concatenate([b, a], axis=0))
                for a, b in zip((own, rate), theirs)
            )
        if plan.paired:
            low, high = ([x[:, :sub] for x in (own, rate)], [x[:, sub:] for x in (own, rate)])
            mine = [jnp.where(half == 0, a, b) for a, b in zip(low, high)]
            inner = [jnp.where(half == 0, b, a) for a, b in zip(low, high)]
            outer = unpack(lax.ppermute(pack(*mine), AXES, plan.swaps(True)), *mine)
            rates = jnp.where(half == 0, jnp.concatenate([outer[1], rate], axis=1), jnp.concatenate([rate, outer[1]], axis=1))
            return (inner[0], mine[0], outer[0]), rates
        both = jnp.concatenate([own, rate[:, :, None, :]], axis=2)
    else:
        both = jnp.concatenate([own, rate[:, :, None, :]], axis=2)
        at = lax.axis_index("lvl") // plan.parts_y
        at = jnp.where(gx % 2 == 0, at, plan.parts_x - 1 - at) * plan.sub_x
        both = lax.dynamic_slice_in_dim(both, at, plan.sub_x, axis=0)
    both = lax.dynamic_slice_in_dim(both, half * sub, sub, axis=1)
    strips = exchange(both[None], plan)
    return [x[0, :, :, :-1] for x in strips], jnp.concatenate([x[0, :, :, -1] for x in strips], axis=1)


def exchange(states, plan):
    if plan.paired:
        return lax.ppermute(states, AXES, plan.swaps(False)), states, lax.ppermute(states, AXES, plan.swaps(True))
    if not plan.closed:
        before = lax.ppermute(states[:, -SWEEPS:], AXES, plan.shifts(1, 0))
        after = lax.ppermute(states[:, :SWEEPS], AXES, plan.shifts(-1, 0))
        states = jnp.concatenate([before, states, after], axis=1)
    before = lax.ppermute(states[:, :, -SWEEPS:], AXES, plan.shifts(0, 1))
    after = lax.ppermute(states[:, :, :SWEEPS], AXES, plan.shifts(0, -1))
    return before, states, after


def halves(x):
    high = x.astype(jnp.bfloat16)
    return high, (x - high.astype(jnp.float32)).astype(jnp.bfloat16)


def product(matrix, x):
    dot = functools.partial(jnp.dot, preferred_element_type=jnp.float32)
    n = matrix.shape[0] // 2
    high, low = halves(x)
    first = dot(matrix, high)
    return first[:n] + (first[n:] + dot(matrix[:n], low))


def level_pass(strips, env, plan, node, inflow_in, inflow_out, kept_old, kept_new, out, fresh):
    u, c, chem, va, vb, wx, wy, wu, rhs, rden = env["scratch"]
    first = va
    if fresh is not None:
        first, wx, wy, wu, rhs, rden = fresh[:6]
    rate, mask, half_d, loss, mats = env["rate"], env["mask"], env["half_d"], env["loss"], env["mats"]
    fields, nz = u.shape[2:]
    rx, ry = plan.core_x, plan.core_y
    hd = half_d[...]
    base = 1 if plan.closed else 0

    def conduct(value):
        return hd + hd * (value * value)

    starts = [0, strips[0].shape[1], strips[0].shape[1] + strips[1].shape[1]]
    if plan.paired:
        side = env["side"][0]
        starts[0], starts[2] = (1 - side) * starts[2], side * starts[2]

    def widen(x, carry):
        for at, strip in zip(starts, strips):
            for y in range(strip.shape[1]):
                value = strip[x, y]
                u[x + base, at + y] = value
                c[x + base, at + y] = conduct(value)
        return carry

    lax.fori_loop(0, strips[0].shape[0], widen, 0)

    lane = lax.broadcasted_iota(jnp.int32, (fields, nz), 1)
    bottom, top = lane == 0, lane == nz - 1
    lr = loss[...]
    advance = node < STEPS

    block = next(n for n in (BLOCK, 4, 2, 1) if rx % n == 0 and (n % 2 == 0 or rx % 2))

    def setup(x0, n):
        rows = range(n)
        u_here, u_next = [u[x0 + j + 1, 0] for j in rows], [u[x0 + j + 1, 1] for j in rows]
        c_here, c_next = [c[x0 + j + 1, 0] for j in rows], [c[x0 + j + 1, 1] for j in rows]
        wy_next = [c_here[j] + c_next[j] for j in rows]
        for y in range(ry):
            Y = y + 1
            u_prev, u_here, u_next = u_here, u_next, [u[x0 + j + 1, Y + 1] for j in rows]
            c_here, c_next = c_next, [c[x0 + j + 1, Y + 1] for j in rows]
            wy_prev, wy_next = wy_next, [c_here[j] + c_next[j] for j in rows]
            u_rows = [u[x0, Y]] + u_here + [u[x0 + n + 1, Y]]
            c_rows = [c[x0, Y]] + c_here + [c[x0 + n + 1, Y]]
            wx_rows = [c_rows[j] + c_rows[j + 1] for j in range(n + 1)]
            for j in rows:
                x, here = x0 + j, u_here[j]
                below = jnp.where(bottom, 0.0, pltpu.roll(here, 1, 1))
                above = jnp.where(top, 0.0, pltpu.roll(here, nz - 1, 1))
                w_low = c_here[j] + conduct(below)
                w_up = c_here[j] + conduct(above)
                weights = ((wx_rows[j] + wx_rows[j + 1]) + (wy_prev[j] + wy_next[j])) + (w_low + w_up)
                near = (
                    (wx_rows[j] * u_rows[j] + wx_rows[j + 1] * u_rows[j + 2])
                    + (wy_prev[j] * u_prev[j] + wy_next[j] * u_next[j])
                    + (w_low * below + w_up * above)
                )
                factor = jnp.broadcast_to(rate[x, pl.ds(y, 1), :], (fields, nz))
                made = factor * chem[1, j, y]
                drop = factor * (lr + chem[0, j, y]) + weights
                if advance:
                    source = here + inflow_in[x, y] if inflow_in is not None else here
                if inflow_out is not None or kept_new is not None:
                    half_t = 0.5 * (near + made - drop * here)
                if inflow_out is not None:
                    inflow_out[x, y] = kept_old[x, y] + (half_t - here)
                if kept_new is not None:
                    kept_new[x, y] = half_t + source
                if advance:
                    right = source + made
                    inverse = (mask[0, x] * mask[1, y]) / (1.0 + drop)
                    rhs[x, y] = right
                    rden[x, y] = inverse
                    wx[x + 1, y] = wx_rows[j + 1]
                    wy[x, y] = wy_next[j]
                    wu[x, y] = jnp.where(top, 0.0, w_up)
                    first[x + 1, y] = (right + near) * inverse

    def rows_of(i, carry):
        x0 = block * i
        for q in range(0, block, 2):
            some = range(q, min(q + 2, block))
            value = jnp.concatenate([u[x0 + k + 1, 1 : 1 + ry].reshape(ry * fields, nz) for k in some], axis=1)
            for j, result in enumerate((product(mats[0], value * value), product(mats[1], value))):
                for k in some:
                    chem[j, k] = result[:, (k - q) * nz : (k - q + 1) * nz].reshape(ry, fields, nz)
        setup(x0, block)
        return carry

    lax.fori_loop(0, rx // block, rows_of, 0)
    if not advance:
        return
    if plan.closed:
        for y in range(ry):
            wx[0, y] = c[0, y + 1] + c[1, y + 1]
    sweeps(plan, first, va, vb, wx, wy, wu, rhs, rden, out)


def first_pass(env, plan, inflow, kept_new, out, fresh):
    va, vb, rhs = env["scratch"][3], env["scratch"][4], env["scratch"][8]
    first, wx, wy, wu, right, rden, kept = fresh

    def add(x, carry):
        for y in range(plan.core_y):
            more = inflow[x, y]
            rhs[x, y] = right[x, y] + more
            va[x + 1, y] = first[x + 1, y] + more * rden[x, y]
            if kept_new is not None:
                kept_new[x, y] = kept[x, y] + more
        return carry

    lax.fori_loop(0, plan.core_x, add, 0)
    sweeps(plan, va, va, vb, wx, wy, wu, rhs, rden, out)


def sweeps(plan, first, va, vb, wx, wy, wu, rhs, rden, out):
    nz = vb.shape[3]
    rx, ry = plan.core_x, plan.core_y
    shrink = 0 if plan.closed else 1
    old, new, spare = first, vb, va
    for k in range(1, SWEEPS):
        lead = k * shrink
        count = rx - 2 * lead
        n = next(n for n in (16, 8, 4, 2, 1) if count % n == 0)

        def sweep(i, carry, k=k, old=old, new=new, lead=lead, n=n):
            x = lead + n * i
            X = x + 1
            v_here = [old[X + j, k - 1] for j in range(n)]
            v_next = [old[X + j, k] for j in range(n)]
            w_next = [wy[x + j, k - 1] for j in range(n)]
            for y in range(k, ry - k):
                v_prev, v_here, v_next = v_here, v_next, [old[X + j, y + 1] for j in range(n)]
                w_prev, w_next = w_next, [wy[x + j, y] for j in range(n)]
                rows = [old[X - 1, y]] + v_here + [old[X + n, y]]
                faces = [wx[X - 1 + j, y] for j in range(n + 1)]
                for j in range(n):
                    w_up = wu[x + j, y]
                    near = (
                        (faces[j] * rows[j] + faces[j + 1] * rows[j + 2])
                        + (w_prev[j] * v_prev[j] + w_next[j] * v_next[j])
                        + (pltpu.roll(w_up * v_here[j], 1, 1) + w_up * pltpu.roll(v_here[j], nz - 1, 1))
                    )
                    value = (rhs[x + j, y] + near) * rden[x + j, y]
                    if k == SWEEPS - 1:
                        out[x + j - lead, y - k] = value
                    else:
                        new[X + j, y] = value
            return carry

        lax.fori_loop(0, count // n, sweep, 0)
        old, new, spare = new, spare, new


def wave(diagonal, group, plan, fields, nz, strips, inflow, common, kept, cache):
    levels = plan.levels
    going = [p for p in group if diagonal - p < STEPS]
    keepers = [p for p in going if p < levels - 1]
    old = [p for p in group if 0 < diagonal - p and p < levels - 1]
    emits = group[-1] in old
    core = (plan.core_x, plan.core_y, fields, nz)
    sources, where = [], {}
    for p in group:
        if p == diagonal and p > 0:
            continue
        arrays, index = strips[p]
        if not (sources and sources[-1] is arrays[-1]):
            sources += list(arrays)
        where[p] = (len(sources) - 3, index)
    n_src = len(sources)
    extra = [] if inflow is None else [inflow]
    makes = diagonal == 0
    shared = list(cache) if diagonal > 0 and diagonal in group else []

    def kernel(*refs):
        refs = list(refs)
        take = lambda n: [refs.pop(0) for _ in range(n)]
        src = take(n_src)
        rate_ref, mask_ref, side_ref, half_ref, loss_ref, mats_ref = take(6)
        old_refs = dict(zip(old, take(len(old))))
        in_refs = take(len(extra))
        shared_refs = take(len(shared))
        state_refs = take(1) if going else []
        new_refs = dict(zip(keepers, take(len(keepers))))
        out_refs = take(1) if emits else []
        made_refs = take(6) if makes else []
        held = refs.pop(-1)
        u, c, _, va, vb = refs[:5]
        env = {"scratch": refs, "rate": rate_ref, "mask": mask_ref, "side": side_ref, "half_d": half_ref, "loss": loss_ref, "mats": mats_ref}
        if plan.closed:
            for x in (0, plan.wide_x - 1):
                for y in range(plan.wide_y):
                    u[x, y] = jnp.zeros((fields, nz), jnp.float32)
                    c[x, y] = half_ref[...]
                for y in range(plan.core_y):
                    va[x, y] = jnp.zeros((fields, nz), jnp.float32)
                    vb[x, y] = jnp.zeros((fields, nz), jnp.float32)
                    if makes:
                        made_refs[0][x, y] = jnp.zeros((fields, nz), jnp.float32)
        for p in group:
            node = diagonal - p
            inflow_in = None if p == 0 or node == STEPS else (in_refs[0] if p == group[0] else held)
            inflow_out = None if p not in old else (out_refs[0] if p == group[-1] else held)
            out = state_refs[0].at[going.index(p)] if p in going else None
            if node == 0 and p > 0:
                first_pass(env, plan, inflow_in, new_refs.get(p), out, shared_refs)
                continue
            at, index = where[p]
            level_pass(
                [r.at[index] for r in src[at : at + 3]], env, plan, node, inflow_in, inflow_out,
                old_refs.get(p), new_refs.get(p), out, made_refs if makes else None,
            )

    vmem = pl.BlockSpec(memory_space=pltpu.VMEM)
    smem = pl.BlockSpec(memory_space=pltpu.SMEM)
    f32 = jnp.float32
    operands = sources + list(common) + [kept[p] for p in old] + extra + shared
    in_specs = [vmem] * n_src + [vmem, smem, smem, vmem, vmem, vmem] + [vmem] * (len(old) + len(extra) + len(shared))
    out_shape = [jax.ShapeDtypeStruct((len(going), plan.sub_x, plan.sub_y, fields, nz), f32)] if going else []
    out_shape += [jax.ShapeDtypeStruct(core, f32)] * (len(keepers) + emits)
    cells = core[0] * core[1] * fields * nz
    wide = (plan.wide_x, plan.wide_y, fields, nz)
    tall = (plan.wide_x,) + core[1:]
    chem = (2, BLOCK) + core[1:]
    if makes:
        out_shape += [jax.ShapeDtypeStruct(shape, f32) for shape in (tall, tall, core, core, core, core)]
    shapes = [wide, wide, chem, tall, tall, tall, core, core, core, core, core]
    results = list(pl.pallas_call(
        kernel,
        out_shape=out_shape,
        in_specs=in_specs,
        out_specs=[vmem] * len(out_shape),
        scratch_shapes=[pltpu.VMEM(s, f32) for s in shapes],
        compiler_params=pltpu.CompilerParams(vmem_limit_bytes=30 * 2**20),
        cost_estimate=pl.CostEstimate(flops=150 * cells * len(group), bytes_accessed=8 * cells * len(group), transcendentals=0),
        name="wave%d_%d" % (diagonal, group[0]),
    )(*operands))
    states = results.pop(0) if going else None
    held = dict(zip(keepers, results))
    if makes:
        cache.extend(results[-6:] + [held[0]])
    return going, states, held, results[-1] if emits else None


def inside_mask(plan):
    part, gx, gy = (lax.axis_index(a) for a in AXES)
    offsets = jnp.arange(max(plan.core_x, plan.core_y))
    cols = (gy * plan.parts_y + part % plan.parts_y) * plan.sub_y + offsets - RIM
    if plan.closed:
        rows = offsets
    else:
        half = part // plan.parts_y
        half = jnp.where(gx % 2 == 0, half, plan.parts_x - 1 - half)
        rows = (gx * plan.parts_x + half) * plan.sub_x + offsets - RIM
    row_ok = (rows >= 0) & (rows < plan.rows * plan.gx)
    col_ok = (cols >= 0) & (cols < plan.cols * plan.gy)
    return jnp.stack([row_ok, col_ok]).astype(jnp.float32)


def matrix_halves(x):
    high = lax.reduce_precision(x, 8, 7)
    return high, x - high


def gather_finals(finals, plan):
    part, gx = lax.axis_index("lvl"), lax.axis_index("gx")
    if not plan.closed:
        parts = lax.all_to_all(jnp.stack(finals), "lvl", 0, 0, tiled=True)
        parts = parts.reshape((plan.parts_x, plan.parts_y) + parts.shape[1:])
        parts = jnp.where(gx % 2 == 0, parts, parts[::-1])
        return jnp.transpose(parts, (0, 2, 1, 3, 4, 5)).reshape((plan.rows, plan.cols) + parts.shape[4:])
    whole = jnp.stack(finals)
    whole = lax.dynamic_slice_in_dim(whole, gx * plan.rows, plan.rows, axis=1)
    n = plan.parts_y
    group = part // n
    column = part % n
    blocks = [None] * n
    got = [lax.dynamic_index_in_dim(whole, part, 0, keepdims=False)]
    for r in range(1, n):
        pairs = [(p, p // n * n + (p % n + r) % n) for p in range(plan.levels)]
        theirs = lax.dynamic_index_in_dim(whole, group * n + (column + r) % n, 0, keepdims=False)
        got.append(lax.ppermute(theirs, "lvl", pairs))
    stack = jnp.stack(got)
    order = jnp.stack([lax.dynamic_index_in_dim(stack, (column - k) % n, 0, keepdims=False) for k in range(n)], axis=1)
    return order.reshape((plan.rows, plan.cols) + order.shape[3:])


def grouped(diagonal, active):
    groups = [[p] for p in active]
    if diagonal - active[0] == STEPS and len(groups) > 2:
        groups[:2] = [groups[0] + groups[1]]
    return groups


def on_device(initial, rate_factor, diffusivity, loss_rate, quench, formation):
    fields, rows, cols, nz = initial.shape
    plan = Plan(rows, cols)
    levels = plan.levels

    started, rate = columns(jnp.transpose(initial, (1, 2, 0, 3)), rate_factor, plan)
    started = [x[None] for x in started]
    rate = rate[:, 1:-1] if plan.closed else rate[1:-1, 1:-1]
    mask = inside_mask(plan)

    reacting = (jnp.arange(fields) < REACT).astype(jnp.float32)
    half_d = jnp.broadcast_to(0.5 * diffusivity[:, None], (fields, nz))
    loss = jnp.broadcast_to((reacting * loss_rate)[:, None], (fields, nz))
    eye = jnp.eye(plan.core_y, dtype=jnp.float32)
    mats = []
    for matrix in ((reacting * loss_rate)[:, None] * quench, reacting[:, None] * formation):
        mats.append(jnp.concatenate([jnp.kron(eye, m) for m in matrix_halves(matrix)], axis=0))
    side = (lax.axis_index("lvl") % plan.parts_y).astype(jnp.int32)[None]
    common = [rate, mask, side, half_d, loss, jnp.stack(mats).astype(jnp.bfloat16)]

    strips, kept, finals, cache = {}, {}, {}, []
    for diagonal in range(levels + STEPS - 1):
        if diagonal < levels:
            strips[diagonal] = (started, 0) if diagonal == 0 else None
        active = [p for p in sorted(strips) if diagonal - p < STEPS + (p < levels - 1)]
        inflow, fresh, held = None, {}, {}
        for group in grouped(diagonal, active):
            going, states, keeps, inflow = wave(diagonal, group, plan, fields, nz, strips, inflow, common, kept, cache)
            held.update(keeps)
            for i, p in enumerate(going):
                if diagonal - p + 1 == STEPS:
                    finals[p] = states[i]
            if going and not (diagonal - going[0] + 1 == STEPS and going[0] == levels - 1):
                arrays = exchange(states, plan)
                fresh.update({p: (arrays, i) for i, p in enumerate(going)})
        strips, kept = fresh, held
    tile = gather_finals([finals[p] for p in range(levels)], plan)
    return jnp.transpose(tile, (2, 0, 1, 3))[None]


def solution(mesh):
    in_specs = (P(None, "gx", "gy", None), P("gx", "gy", None), P(), P(), P(), P())
    out_specs = P("lvl", None, "gx", "gy", None)
    return jax.shard_map(
        on_device, mesh=mesh, in_specs=in_specs, out_specs=out_specs, check_vma=False
    )
```

```python
import functools

import jax
import jax.numpy as jnp
from jax import lax
from jax.experimental import pallas as pl
from jax.experimental.pallas import tpu as pltpu
from jax.sharding import PartitionSpec as P

REACT = 11
STEPS = 4
SWEEPS = 4
RIM = SWEEPS - 1
BLOCK = 4
AXES = ("lvl", "gx", "gy")


class Plan:
    def __init__(self, rows, cols):
        self.levels, self.gx, self.gy = (lax.axis_size(a) for a in AXES)
        self.rows, self.cols = rows, cols
        self.closed = self.gx <= 2
        parts = self.levels
        if self.closed:
            self.parts_x, self.parts_y = 1, 1
            while parts % (2 * self.parts_y) == 0 and cols // (2 * self.parts_y) >= SWEEPS:
                self.parts_y *= 2
            self.sub_x, self.wide_x = rows * self.gx, rows * self.gx + 2
        else:
            self.parts_x = 1
            while self.parts_x * self.parts_x < parts:
                self.parts_x *= 2
            self.parts_y = parts // self.parts_x
            assert self.parts_x * self.parts_y == parts and rows % self.parts_x == 0
            self.sub_x, self.wide_x = rows // self.parts_x, rows // self.parts_x + 2 * SWEEPS
        assert cols % self.parts_y == 0
        self.sub_y = cols // self.parts_y
        assert min(self.sub_x, self.sub_y) >= SWEEPS
        self.wide_y = self.sub_y + 2 * SWEEPS
        self.core_x, self.core_y = self.wide_x - 2, self.wide_y - 2
        self.paired = self.closed and self.parts_y == 2 and self.sub_y == SWEEPS

    def spot(self, part, gx, gy):
        at_y = gy * self.parts_y + part % self.parts_y
        if self.closed:
            return gx, part // self.parts_y, at_y
        half = part // self.parts_y
        half = half if gx % 2 == 0 else self.parts_x - 1 - half
        return gx * self.parts_x + half, 0, at_y

    def devices(self):
        found = {}
        for part in range(self.levels):
            for gx in range(self.gx):
                for gy in range(self.gy):
                    found[self.spot(part, gx, gy)] = (part * self.gx + gx) * self.gy + gy
        return found

    def column(self, device):
        return device // (self.gx * self.gy) % self.parts_y

    def swaps(self, outside):
        return sorted(
            [(a, b) for a, b in self.shifts(0, 1) if self.column(a) == (1 if outside else 0)]
            + [(a, b) for a, b in self.shifts(0, -1) if self.column(a) == (0 if outside else 1)]
        )

    def shifts(self, dx, dy):
        found = self.devices()
        there = lambda s: (s[0] + dx, s[1], s[2] + dy)
        return [(d, found[there(s)]) for s, d in sorted(found.items()) if there(s) in found]


def columns(initial, rate, plan):
    half = lax.axis_index("lvl") % plan.parts_y
    gx = lax.axis_index("gx")
    own = jnp.transpose(initial, (1, 2, 0, 3))
    sub, nz = plan.sub_y, own.shape[-1]
    if plan.closed:
        def pack(x, r):
            return jnp.concatenate([x.reshape(-1, nz), r.reshape(-1, nz)], axis=0)

        def unpack(packed, x, r):
            return packed[: x.size // nz].reshape(x.shape), packed[x.size // nz :].reshape(r.shape)

        if plan.gx == 2:
            theirs = [lax.ppermute(x, "gx", [(0, 1), (1, 0)]) for x in (initial, rate)]
            theirs[0] = jnp.transpose(theirs[0], (1, 2, 0, 3))
            own, rate = (
                jnp.where(gx == 0, jnp.concatenate([a, b], axis=0), jnp.concatenate([b, a], axis=0))
                for a, b in zip((own, rate), theirs)
            )
        if plan.paired:
            low, high = ([x[:, :sub] for x in (own, rate)], [x[:, sub:] for x in (own, rate)])
            mine = [jnp.where(half == 0, a, b) for a, b in zip(low, high)]
            inner = [jnp.where(half == 0, b, a) for a, b in zip(low, high)]
            outer = unpack(lax.ppermute(pack(*mine), AXES, plan.swaps(True)), *mine)
            rates = jnp.where(half == 0, jnp.concatenate([outer[1], rate], axis=1), jnp.concatenate([rate, outer[1]], axis=1))
            return (inner[0], mine[0], outer[0]), rates
        both = jnp.concatenate([own, rate[:, :, None, :]], axis=2)
    else:
        both = jnp.concatenate([own, rate[:, :, None, :]], axis=2)
        at = lax.axis_index("lvl") // plan.parts_y
        at = jnp.where(gx % 2 == 0, at, plan.parts_x - 1 - at) * plan.sub_x
        both = lax.dynamic_slice_in_dim(both, at, plan.sub_x, axis=0)
    both = lax.dynamic_slice_in_dim(both, half * sub, sub, axis=1)
    strips = exchange(both[None], plan)
    return [x[0, :, :, :-1] for x in strips], jnp.concatenate([x[0, :, :, -1] for x in strips], axis=1)


def exchange(states, plan):
    if plan.paired:
        return lax.ppermute(states, AXES, plan.swaps(False)), states, lax.ppermute(states, AXES, plan.swaps(True))
    if not plan.closed:
        before = lax.ppermute(states[:, -SWEEPS:], AXES, plan.shifts(1, 0))
        after = lax.ppermute(states[:, :SWEEPS], AXES, plan.shifts(-1, 0))
        states = jnp.concatenate([before, states, after], axis=1)
    before = lax.ppermute(states[:, :, -SWEEPS:], AXES, plan.shifts(0, 1))
    after = lax.ppermute(states[:, :, :SWEEPS], AXES, plan.shifts(0, -1))
    return before, states, after


def halves(x):
    high = x.astype(jnp.bfloat16)
    return high, (x - high.astype(jnp.float32)).astype(jnp.bfloat16)


def product(matrix, x):
    dot = functools.partial(jnp.dot, preferred_element_type=jnp.float32)
    n = matrix.shape[0] // 2
    high, low = halves(x)
    first = dot(matrix, high)
    return first[:n] + (first[n:] + dot(matrix[:n], low))


def level_pass(strips, env, plan, node, inflow_in, inflow_out, kept_old, kept_new, out, fresh):
    u, c, chem, va, vb, wx, wy, wu, rhs, rden = env["scratch"]
    first = va
    if fresh is not None:
        first, wx, wy, wu, rhs, rden = fresh[:6]
    rate, mask, half_d, loss, mats = env["rate"], env["mask"], env["half_d"], env["loss"], env["mats"]
    fields, nz = u.shape[2:]
    rx, ry = plan.core_x, plan.core_y
    hd = half_d[...]
    base = 1 if plan.closed else 0

    def conduct(value):
        return hd + hd * (value * value)

    starts = [0, strips[0].shape[1], strips[0].shape[1] + strips[1].shape[1]]
    if plan.paired:
        side = env["side"][0]
        starts[0], starts[2] = (1 - side) * starts[2], side * starts[2]

    def widen(x, carry):
        for at, strip in zip(starts, strips):
            for y in range(strip.shape[1]):
                value = strip[x, y]
                u[x + base, at + y] = value
                c[x + base, at + y] = conduct(value)
        return carry

    lax.fori_loop(0, strips[0].shape[0], widen, 0)

    lane = lax.broadcasted_iota(jnp.int32, (fields, nz), 1)
    bottom, top = lane == 0, lane == nz - 1
    lr = loss[...]
    advance = node < STEPS

    block = next(n for n in (BLOCK, 4, 2, 1) if rx % n == 0 and (n % 2 == 0 or rx % 2))

    def setup(x0, n):
        rows = range(n)
        u_here, u_next = [u[x0 + j + 1, 0] for j in rows], [u[x0 + j + 1, 1] for j in rows]
        c_here, c_next = [c[x0 + j + 1, 0] for j in rows], [c[x0 + j + 1, 1] for j in rows]
        wy_next = [c_here[j] + c_next[j] for j in rows]
        for y in range(ry):
            Y = y + 1
            u_prev, u_here, u_next = u_here, u_next, [u[x0 + j + 1, Y + 1] for j in rows]
            c_here, c_next = c_next, [c[x0 + j + 1, Y + 1] for j in rows]
            wy_prev, wy_next = wy_next, [c_here[j] + c_next[j] for j in rows]
            u_rows = [u[x0, Y]] + u_here + [u[x0 + n + 1, Y]]
            c_rows = [c[x0, Y]] + c_here + [c[x0 + n + 1, Y]]
            wx_rows = [c_rows[j] + c_rows[j + 1] for j in range(n + 1)]
            for j in rows:
                x, here = x0 + j, u_here[j]
                below = jnp.where(bottom, 0.0, pltpu.roll(here, 1, 1))
                above = jnp.where(top, 0.0, pltpu.roll(here, nz - 1, 1))
                w_low = c_here[j] + conduct(below)
                w_up = c_here[j] + conduct(above)
                weights = ((wx_rows[j] + wx_rows[j + 1]) + (wy_prev[j] + wy_next[j])) + (w_low + w_up)
                near = (
                    (wx_rows[j] * u_rows[j] + wx_rows[j + 1] * u_rows[j + 2])
                    + (wy_prev[j] * u_prev[j] + wy_next[j] * u_next[j])
                    + (w_low * below + w_up * above)
                )
                factor = jnp.broadcast_to(rate[x, pl.ds(y, 1), :], (fields, nz))
                made = factor * chem[1, j, y]
                drop = factor * (lr + chem[0, j, y]) + weights
                if advance:
                    source = here + inflow_in[x, y] if inflow_in is not None else here
                if inflow_out is not None or kept_new is not None:
                    half_t = 0.5 * (near + made - drop * here)
                if inflow_out is not None:
                    inflow_out[x, y] = kept_old[x, y] + (half_t - here)
                if kept_new is not None:
                    kept_new[x, y] = half_t + source
                if advance:
                    right = source + made
                    inverse = (mask[0, x] * mask[1, y]) / (1.0 + drop)
                    rhs[x, y] = right
                    rden[x, y] = inverse
                    wx[x + 1, y] = wx_rows[j + 1]
                    wy[x, y] = wy_next[j]
                    wu[x, y] = jnp.where(top, 0.0, w_up)
                    first[x + 1, y] = (right + near) * inverse

    def rows_of(i, carry):
        x0 = block * i
        for q in range(0, block, 2):
            some = range(q, min(q + 2, block))
            value = jnp.concatenate([u[x0 + k + 1, 1 : 1 + ry].reshape(ry * fields, nz) for k in some], axis=1)
            for j, result in enumerate((product(mats[0], value * value), product(mats[1], value))):
                for k in some:
                    chem[j, k] = result[:, (k - q) * nz : (k - q + 1) * nz].reshape(ry, fields, nz)
        setup(x0, block)
        return carry

    lax.fori_loop(0, rx // block, rows_of, 0)
    if not advance:
        return
    if plan.closed:
        for y in range(ry):
            wx[0, y] = c[0, y + 1] + c[1, y + 1]
    sweeps(plan, first, va, vb, wx, wy, wu, rhs, rden, out)


def first_pass(env, plan, inflow, kept_new, out, fresh):
    va, vb, rhs = env["scratch"][3], env["scratch"][4], env["scratch"][8]
    first, wx, wy, wu, right, rden, kept = fresh

    def add(x, carry):
        for y in range(plan.core_y):
            more = inflow[x, y]
            rhs[x, y] = right[x, y] + more
            va[x + 1, y] = first[x + 1, y] + more * rden[x, y]
            if kept_new is not None:
                kept_new[x, y] = kept[x, y] + more
        return carry

    lax.fori_loop(0, plan.core_x, add, 0)
    sweeps(plan, va, va, vb, wx, wy, wu, rhs, rden, out)


def sweeps(plan, first, va, vb, wx, wy, wu, rhs, rden, out):
    nz = vb.shape[3]
    rx, ry = plan.core_x, plan.core_y
    shrink = 0 if plan.closed else 1
    old, new, spare = first, vb, va
    for k in range(1, SWEEPS):
        lead = k * shrink
        count = rx - 2 * lead
        n = next(n for n in (16, 8, 4, 2, 1) if count % n == 0)

        def sweep(i, carry, k=k, old=old, new=new, lead=lead, n=n):
            x = lead + n * i
            X = x + 1
            v_here = [old[X + j, k - 1] for j in range(n)]
            v_next = [old[X + j, k] for j in range(n)]
            w_next = [wy[x + j, k - 1] for j in range(n)]
            for y in range(k, ry - k):
                v_prev, v_here, v_next = v_here, v_next, [old[X + j, y + 1] for j in range(n)]
                w_prev, w_next = w_next, [wy[x + j, y] for j in range(n)]
                rows = [old[X - 1, y]] + v_here + [old[X + n, y]]
                faces = [wx[X - 1 + j, y] for j in range(n + 1)]
                for j in range(n):
                    w_up = wu[x + j, y]
                    near = (
                        (faces[j] * rows[j] + faces[j + 1] * rows[j + 2])
                        + (w_prev[j] * v_prev[j] + w_next[j] * v_next[j])
                        + (pltpu.roll(w_up * v_here[j], 1, 1) + w_up * pltpu.roll(v_here[j], nz - 1, 1))
                    )
                    value = (rhs[x + j, y] + near) * rden[x + j, y]
                    if k == SWEEPS - 1:
                        out[x + j - lead, y - k] = value
                    else:
                        new[X + j, y] = value
            return carry

        lax.fori_loop(0, count // n, sweep, 0)
        old, new, spare = new, spare, new


def wave(diagonal, group, plan, fields, nz, strips, inflow, common, kept, cache):
    levels = plan.levels
    going = [p for p in group if diagonal - p < STEPS]
    keepers = [p for p in going if p < levels - 1]
    old = [p for p in group if 0 < diagonal - p and p < levels - 1]
    emits = group[-1] in old
    core = (plan.core_x, plan.core_y, fields, nz)
    sources, where = [], {}
    for p in group:
        if p == diagonal and p > 0:
            continue
        arrays, index = strips[p]
        if not (sources and sources[-1] is arrays[-1]):
            sources += list(arrays)
        where[p] = (len(sources) - 3, index)
    n_src = len(sources)
    extra = [] if inflow is None else [inflow]
    makes = diagonal == 0
    shared = list(cache) if diagonal > 0 and diagonal in group else []

    def kernel(*refs):
        refs = list(refs)
        take = lambda n: [refs.pop(0) for _ in range(n)]
        src = take(n_src)
        rate_ref, mask_ref, side_ref, half_ref, loss_ref, mats_ref = take(6)
        old_refs = dict(zip(old, take(len(old))))
        in_refs = take(len(extra))
        shared_refs = take(len(shared))
        state_refs = take(1) if going else []
        new_refs = dict(zip(keepers, take(len(keepers))))
        out_refs = take(1) if emits else []
        made_refs = take(6) if makes else []
        held = refs.pop(-1)
        u, c, _, va, vb = refs[:5]
        env = {"scratch": refs, "rate": rate_ref, "mask": mask_ref, "side": side_ref, "half_d": half_ref, "loss": loss_ref, "mats": mats_ref}
        if plan.closed:
            for x in (0, plan.wide_x - 1):
                for y in range(plan.wide_y):
                    u[x, y] = jnp.zeros((fields, nz), jnp.float32)
                    c[x, y] = half_ref[...]
                for y in range(plan.core_y):
                    va[x, y] = jnp.zeros((fields, nz), jnp.float32)
                    vb[x, y] = jnp.zeros((fields, nz), jnp.float32)
                    if makes:
                        made_refs[0][x, y] = jnp.zeros((fields, nz), jnp.float32)
        for p in group:
            node = diagonal - p
            inflow_in = None if p == 0 or node == STEPS else (in_refs[0] if p == group[0] else held)
            inflow_out = None if p not in old else (out_refs[0] if p == group[-1] else held)
            out = state_refs[0].at[going.index(p)] if p in going else None
            if node == 0 and p > 0:
                first_pass(env, plan, inflow_in, new_refs.get(p), out, shared_refs)
                continue
            at, index = where[p]
            level_pass(
                [r.at[index] for r in src[at : at + 3]], env, plan, node, inflow_in, inflow_out,
                old_refs.get(p), new_refs.get(p), out, made_refs if makes else None,
            )

    vmem = pl.BlockSpec(memory_space=pltpu.VMEM)
    smem = pl.BlockSpec(memory_space=pltpu.SMEM)
    f32 = jnp.float32
    operands = sources + list(common) + [kept[p] for p in old] + extra + shared
    in_specs = [vmem] * n_src + [vmem, smem, smem, vmem, vmem, vmem] + [vmem] * (len(old) + len(extra) + len(shared))
    out_shape = [jax.ShapeDtypeStruct((len(going), plan.sub_x, plan.sub_y, fields, nz), f32)] if going else []
    out_shape += [jax.ShapeDtypeStruct(core, f32)] * (len(keepers) + emits)
    cells = core[0] * core[1] * fields * nz
    wide = (plan.wide_x, plan.wide_y, fields, nz)
    tall = (plan.wide_x,) + core[1:]
    chem = (2, BLOCK) + core[1:]
    if makes:
        out_shape += [jax.ShapeDtypeStruct(shape, f32) for shape in (tall, tall, core, core, core, core)]
    shapes = [wide, wide, chem, tall, tall, tall, core, core, core, core, core]
    results = list(pl.pallas_call(
        kernel,
        out_shape=out_shape,
        in_specs=in_specs,
        out_specs=[vmem] * len(out_shape),
        scratch_shapes=[pltpu.VMEM(s, f32) for s in shapes],
        compiler_params=pltpu.CompilerParams(vmem_limit_bytes=30 * 2**20),
        cost_estimate=pl.CostEstimate(flops=150 * cells * len(group), bytes_accessed=8 * cells * len(group), transcendentals=0),
        name="wave%d_%d" % (diagonal, group[0]),
    )(*operands))
    states = results.pop(0) if going else None
    held = dict(zip(keepers, results))
    if makes:
        cache.extend(results[-6:] + [held[0]])
    return going, states, held, results[-1] if emits else None


def inside_mask(plan):
    part, gx, gy = (lax.axis_index(a) for a in AXES)
    offsets = jnp.arange(max(plan.core_x, plan.core_y))
    cols = (gy * plan.parts_y + part % plan.parts_y) * plan.sub_y + offsets - RIM
    if plan.closed:
        rows = offsets
    else:
        half = part // plan.parts_y
        half = jnp.where(gx % 2 == 0, half, plan.parts_x - 1 - half)
        rows = (gx * plan.parts_x + half) * plan.sub_x + offsets - RIM
    row_ok = (rows >= 0) & (rows < plan.rows * plan.gx)
    col_ok = (cols >= 0) & (cols < plan.cols * plan.gy)
    return jnp.stack([row_ok, col_ok]).astype(jnp.float32)


def matrix_halves(x):
    high = lax.reduce_precision(x, 8, 7)
    return high, x - high


def gather_finals(finals, plan):
    part, gx = lax.axis_index("lvl"), lax.axis_index("gx")
    if not plan.closed:
        parts = lax.all_to_all(jnp.stack(finals), "lvl", 0, 0, tiled=True)
        parts = parts.reshape((plan.parts_x, plan.parts_y) + parts.shape[1:])
        parts = jnp.where(gx % 2 == 0, parts, parts[::-1])
        return jnp.transpose(parts, (0, 2, 1, 3, 4, 5)).reshape((plan.rows, plan.cols) + parts.shape[4:])
    whole = jnp.stack(finals)
    whole = lax.dynamic_slice_in_dim(whole, gx * plan.rows, plan.rows, axis=1)
    n = plan.parts_y
    group = part // n
    column = part % n
    blocks = [None] * n
    got = [lax.dynamic_index_in_dim(whole, part, 0, keepdims=False)]
    for r in range(1, n):
        pairs = [(p, p // n * n + (p % n + r) % n) for p in range(plan.levels)]
        theirs = lax.dynamic_index_in_dim(whole, group * n + (column + r) % n, 0, keepdims=False)
        got.append(lax.ppermute(theirs, "lvl", pairs))
    stack = jnp.stack(got)
    order = jnp.stack([lax.dynamic_index_in_dim(stack, (column - k) % n, 0, keepdims=False) for k in range(n)], axis=1)
    return order.reshape((plan.rows, plan.cols) + order.shape[3:])


def grouped(diagonal, active):
    groups = [[p] for p in active]
    if diagonal - active[0] == STEPS and len(groups) > 2:
        groups[:2] = [groups[0] + groups[1]]
    return groups


def on_device(initial, rate_factor, diffusivity, loss_rate, quench, formation):
    fields, rows, cols, nz = initial.shape
    plan = Plan(rows, cols)
    levels = plan.levels

    started, rate = columns(initial, rate_factor, plan)
    started = [x[None] for x in started]
    rate = rate[:, 1:-1] if plan.closed else rate[1:-1, 1:-1]
    mask = inside_mask(plan)

    reacting = (jnp.arange(fields) < REACT).astype(jnp.float32)
    half_d = jnp.broadcast_to(0.5 * diffusivity[:, None], (fields, nz))
    loss = jnp.broadcast_to((reacting * loss_rate)[:, None], (fields, nz))
    eye = jnp.eye(plan.core_y, dtype=jnp.float32)
    mats = []
    for matrix in ((reacting * loss_rate)[:, None] * quench, reacting[:, None] * formation):
        mats.append(jnp.concatenate([jnp.kron(eye, m) for m in matrix_halves(matrix)], axis=0))
    side = (lax.axis_index("lvl") % plan.parts_y).astype(jnp.int32)[None]
    common = [rate, mask, side, half_d, loss, jnp.stack(mats).astype(jnp.bfloat16)]

    strips, kept, finals, cache = {}, {}, {}, []
    for diagonal in range(levels + STEPS - 1):
        if diagonal < levels:
            strips[diagonal] = (started, 0) if diagonal == 0 else None
        active = [p for p in sorted(strips) if diagonal - p < STEPS + (p < levels - 1)]
        inflow, fresh, held = None, {}, {}
        for group in grouped(diagonal, active):
            going, states, keeps, inflow = wave(diagonal, group, plan, fields, nz, strips, inflow, common, kept, cache)
            held.update(keeps)
            for i, p in enumerate(going):
                if diagonal - p + 1 == STEPS:
                    finals[p] = states[i]
            if going and not (diagonal - going[0] + 1 == STEPS and going[0] == levels - 1):
                arrays = exchange(states, plan)
                fresh.update({p: (arrays, i) for i, p in enumerate(going)})
        strips, kept = fresh, held
    tile = gather_finals([finals[p] for p in range(levels)], plan)
    return jnp.transpose(tile, (2, 0, 1, 3))[None]


def solution(mesh):
    in_specs = (P(None, "gx", "gy", None), P("gx", "gy", None), P(), P(), P(), P())
    out_specs = P("lvl", None, "gx", "gy", None)
    return jax.shard_map(
        on_device, mesh=mesh, in_specs=in_specs, out_specs=out_specs, check_vma=False
    )
```
